32 devices in a mesh: dp: 8 (over y, x, core), tensor: 4 (over z).
Axes of the slice: x: 2, y: 2, z: 4, core: 2. Of those that a mesh axis runs over, the one named last changes fastest.
Arguments:
- inputs: bfloat16 [18432, 768], P('dp'), may hold values from -6 to 6
- cotangent: bfloat16 [18432, 768], P('dp'), may hold values from -6 to 6, as said below
- row_expert: int32 [18432], P('dp'), may hold values from 0 to 2, as said below
- row_keep: int32 [18432], P('dp'), may hold values from 0 to 1, as said below
- window_resolution: int32 [24], P('dp'), may hold values from 0 to 1, as said below
- attention_norm_gain: float32 [768], replicated, may hold values from 0.5 to 1.5
- attention_norm_bias: float32 [768], replicated, may hold values from -0.6 to 0.6
- qkv_weight: bfloat16 [3, 768, 768], P(None, None, 'tensor'), may hold values from -0.21875 to 0.21875
- qv_bias: float32 [2, 12, 64], P(None, 'tensor'), may hold values from -1.8 to 1.8
- out_weight: bfloat16 [768, 768], P('tensor'), may hold values from -2.5 to 2.5
- out_bias: float32 [768], replicated, may hold values from -0.6 to 0.6
- second_gain: float32 [3, 768], replicated, may hold values from 0.5 to 1.5
- expert_norm_bias: float32 [3, 768], replicated, may hold values from -0.6 to 0.6
- up_weight: bfloat16 [3, 768, 3072], P(None, None, 'tensor'), may hold values from -0.21875 to 0.21875
- up_bias: float32 [3, 3072], P(None, 'tensor'), may hold values from -0.6 to 0.6
- down_weight: bfloat16 [3, 3072, 768], P(None, 'tensor'), may hold values from -0.109375 to 0.109375
- down_bias: float32 [3, 768], replicated, may hold values from -0.6 to 0.6
Outputs:
- layer_out: bfloat16 [18432, 768], P('dp')
- input_rows_gradient: bfloat16 [18432, 768], P('dp')
- attention_gain_gradient: float32 [768], replicated
- grad_first_bias: float32 [768], replicated
- grad_qkv: float32 [3, 768, 768], P(None, 'dp', 'tensor')
- grad_qv_bias: float32 [2, 12, 64], P(None, 'tensor')
- grad_out_weight: float32 [768, 768], P('tensor', 'dp')
- grad_out_bias: float32 [768], replicated
- expert_gain_gradient: float32 [3, 768], replicated
- grad_second_bias: float32 [3, 768], replicated
- grad_up: float32 [3, 768, 3072], P(None, 'dp', 'tensor')
- grad_up_bias: float32 [3, 3072], P(None, 'tensor')
- grad_down: float32 [3, 3072, 768], P(None, 'tensor', 'dp')
- grad_down_bias: float32 [3, 768], replicated
The draws below stay inside these ranges and needn't reach their ends.
Inputs may be any that keep to these rules, and one draw needn't show every extreme that they name: `row_expert`: rows come in windows of 768 slots. A window with window_resolution = 1 holds one pair: 577 image rows, then 1 to 64 text rows, then padding. One with 0 holds two pairs, one in each half of 384 slots, each of 197 image rows, then 1 to 64 text rows, then padding. In some pairs every real row uses expert 2; otherwise image rows use 0 and text rows 1. Padding rows use 1. `row_keep`: 1 on the image and text rows of a pair, 0 on its padding; every pair has padding and its first row is real. `window_resolution`: all windows of one index of dp have the same value. `cotangent`: 0 on every row with row_keep = 0.
All inputs are finite; a program needn't handle non-finite values.
Results may differ from the reference program's by a relative error of at most 0.015.
Values may be sent and summed in bfloat16 or wider, within the bound.
No kernel may reach another device: no remote copies, remote signals or barrier semaphores. Data moves between devices by JAX's collectives and lax.ppermute only.
A program may use at most 256 MiB of HBM per device.

```python
import math
import jax
import jax.numpy as jnp
from jax import lax

D = 768
HEADS = 12
HEAD_DIM = 64
FF = 3072
EXPERTS = 3
S = 768
SEQS = 3
IMG_LO = 197
IMG_HI = 577
TXT = 64
TOKENS = 18432


def sequence_layout(key):
    seq_total = TOKENS // S
    group_total = seq_total // SEQS
    res_key, text_key, merge_key = jax.random.split(jax.random.fold_in(key, 11), 3)
    resolution = jax.random.randint(res_key, (group_total,), 0, 2)
    resolution = jnp.repeat(resolution, SEQS, total_repeat_length=seq_total)
    text_len = jax.random.randint(text_key, (seq_total, 2), 1, TXT + 1)
    merged_flag = jax.random.randint(merge_key, (seq_total, 2), 0, 2)
    position = jnp.arange(S, dtype=jnp.int32)[None, :]
    single = resolution[:, None] == 1
    upper = (position >= S // 2) & jnp.logical_not(single)
    local = position - jnp.where(upper, S // 2, 0)
    image_len = jnp.where(single, IMG_HI, IMG_LO)
    text_rows = jnp.where(upper, text_len[:, 1:2], text_len[:, 0:1])
    merged_rows = jnp.where(upper, merged_flag[:, 1:2], merged_flag[:, 0:1])
    kept_rows = local < image_len + text_rows
    expert_ids = jnp.where(local < image_len, 0, 1)
    expert_ids = jnp.where(kept_rows & (merged_rows == 1), 2, expert_ids)
    return (expert_ids.reshape(-1).astype(jnp.int32), kept_rows.astype(jnp.int32).reshape(-1), resolution.astype(jnp.int32))


def draw_row_expert(key, part):
    return sequence_layout(key)[0]


def draw_row_keep(key, part):
    return sequence_layout(key)[1]


def draw_window_resolution(key, part):
    return sequence_layout(key)[2]


def draw_cotangent(key, part):
    keep_rows = sequence_layout(key)[1].astype(jnp.float32)
    noise = jax.random.truncated_normal(jax.random.fold_in(key, 23), -6.0, 6.0, (TOKENS, D), jnp.float32)
    return (noise * keep_rows[:, None]).astype(jnp.bfloat16)


def shard_levels(stream_key, dims, cuts, smallest, top_value):
    factor_of = 1.0
    for dim, blocks in cuts:
        heights = jax.random.uniform(jax.random.fold_in(jax.random.fold_in(stream_key, 6), dim), (blocks,), jnp.float32, smallest / len(cuts), top_value / len(cuts))
        factor_of = factor_of * jnp.repeat(jnp.exp(heights), dims[dim] // blocks).reshape((-1,) + (1,) * (len(dims) - 1 - dim))
    return factor_of


def normal_values(stream_key, extent, spread, most, shards=(), kind=jnp.bfloat16):
    result = jax.random.normal(stream_key, extent, jnp.float32) * spread
    if len(shards) > 0:
        result = shard_levels(stream_key, extent, shards, -0.22, 0.18) * result
    return jnp.clip(result, min=-most, max=most).astype(kind)


def setup_inputs(seed: int = 0) -> dict:
    key_list = jax.random.split(jax.random.key(seed), 18)
    inputs = normal_values(key_list[0], (TOKENS, D), 1.0, 6.0, ((0, 8),))
    cotangent = draw_cotangent(jax.random.fold_in(key_list[17], 71), 0)
    row_expert = draw_row_expert(jax.random.fold_in(key_list[17], 71), 0)
    row_keep = draw_row_keep(jax.random.fold_in(key_list[17], 71), 0)
    window_resolution = draw_window_resolution(jax.random.fold_in(key_list[17], 71), 0)
    attention_norm_gain = jnp.clip(1.0 + 0.1 * jax.random.normal(key_list[5], (D,), jnp.float32), 0.5, 1.5)
    attention_norm_bias = normal_values(key_list[6], (D,), 0.1, 0.6, (), jnp.float32)
    qkv_weight = normal_values(key_list[7], (3, D, D), D ** -0.5, 0.21875, ((2, 4),))
    qv_bias = normal_values(key_list[8], (2, HEADS, HEAD_DIM), 0.3, 1.8, ((1, 4),), jnp.float32)
    out_weight = normal_values(key_list[9], (D, D), (max(D // 128, 1)) ** -0.5, 2.5, ((0, 4),))
    out_bias = normal_values(key_list[10], (D,), 0.1, 0.6, (), jnp.float32)
    second_gain = jnp.clip(1.0 + 0.1 * jax.random.normal(key_list[11], (EXPERTS, D), jnp.float32), 0.5, 1.5)
    expert_norm_bias = normal_values(key_list[12], (EXPERTS, D), 0.1, 0.6, (), jnp.float32)
    up_weight = normal_values(key_list[13], (EXPERTS, D, FF), D ** -0.5, 0.21875, ((2, 4),))
    up_bias = normal_values(key_list[14], (EXPERTS, FF), 0.1, 0.6, ((1, 4),), jnp.float32)
    down_weight = normal_values(key_list[15], (EXPERTS, FF, D), FF ** -0.5, 0.109375, ((1, 4),))
    down_bias = normal_values(key_list[16], (EXPERTS, D), 0.1, 0.6, (), jnp.float32)
    return dict(inputs=inputs, cotangent=cotangent, row_expert=row_expert, row_keep=row_keep, window_resolution=window_resolution, attention_norm_gain=attention_norm_gain, attention_norm_bias=attention_norm_bias, qkv_weight=qkv_weight, qv_bias=qv_bias, out_weight=out_weight, out_bias=out_bias, second_gain=second_gain, expert_norm_bias=expert_norm_bias, up_weight=up_weight, up_bias=up_bias, down_weight=down_weight, down_bias=down_bias)


epsilon = 1e-05
masked_score = -1000000000.0
highest = lax.Precision.HIGHEST

@jax.custom_vjp
def low(v):
    return lax.optimization_barrier(v.astype(jnp.bfloat16)).astype(jnp.float32)

@jax.custom_vjp
def low_back(v):
    return v

def low_keep(v):
    return (low(v), None)

def low_pass(kept, grad):
    return (grad,)

def back_keep(v):
    return (v, None)

def back_low(kept, grad):
    return (low(grad),)
low.defvjp(low_keep, low_pass)
low_back.defvjp(back_keep, back_low)

def layer_norm(values, gain, shift):
    mean_row = lax.optimization_barrier(jnp.mean(values, -1, keepdims=True))
    centred = values - mean_row
    variance = lax.optimization_barrier(jnp.mean(centred * centred, -1, keepdims=True))
    return centred * lax.rsqrt(variance + epsilon) * gain + shift

def block_forward(params, block_rows, block_expert, block_keep, block_single):
    attention_norm_gain, attention_norm_bias, qkv_weight, qv_bias, out_weight, out_bias, second_gain, expert_norm_bias, up_weight, up_bias, down_weight, down_bias = params
    row_count, model_width = block_rows.shape
    seq_count = row_count // S
    scale_factor = 1.0 / math.sqrt(HEAD_DIM)
    attention_normed = low(layer_norm(block_rows, attention_norm_gain, attention_norm_bias))
    bias_pair = qv_bias.reshape(2, model_width)
    query = low_back(low(jnp.dot(attention_normed, qkv_weight[0], precision=highest) + bias_pair[0]))
    keyed = low_back(low(jnp.dot(attention_normed, qkv_weight[1], precision=highest)))
    valued = low_back(low(jnp.dot(attention_normed, qkv_weight[2], precision=highest) + bias_pair[1]))
    head_shape = (seq_count, S, HEADS, HEAD_DIM)
    scores = jnp.einsum('bqhd,bkhd->bhqk', query.reshape(head_shape), keyed.reshape(head_shape), precision=highest) * scale_factor
    scores = low_back(scores)
    positions = jnp.arange(S, dtype=jnp.int32)
    upper = positions >= S // 2
    same_half = (upper[:, None] == upper[None, :])[None, None, :, :]
    allowed = (block_keep.reshape(seq_count, 1, 1, S) > 0) & (same_half | (block_single.reshape(seq_count, 1, 1, 1) > 0))
    scores = jnp.where(allowed, scores, masked_score)
    probs = low(jax.nn.softmax(scores, axis=-1))
    mixed = jnp.einsum('bhqk,bkhd->bqhd', probs, valued.reshape(head_shape), precision=highest)
    mixed = low_back(low(mixed)).reshape(row_count, model_width)
    attn_out = low_back(jnp.dot(mixed, out_weight, precision=highest) + out_bias)
    residual_hidden = block_rows + attn_out
    expert_normed = low(layer_norm(residual_hidden, second_gain[block_expert], expert_norm_bias[block_expert]))
    expert_total = down_bias[block_expert]
    for expert_id in range(EXPERTS):
        pre_act = low_back(jnp.dot(expert_normed, up_weight[expert_id], precision=highest) + up_bias[expert_id])
        act_out = low(jax.nn.gelu(pre_act, approximate=False))
        select = (block_expert == expert_id).astype(jnp.float32)[:, None]
        expert_total = expert_total + select * jnp.dot(act_out, down_weight[expert_id], precision=highest)
    return residual_hidden + expert_total

def reference(inputs, cotangent, row_expert, row_keep, window_resolution, attention_norm_gain, attention_norm_bias, qkv_weight, qv_bias, out_weight, out_bias, second_gain, expert_norm_bias, up_weight, up_bias, down_weight, down_bias):
    params = tuple((item.astype(jnp.float32) for item in (attention_norm_gain, attention_norm_bias, qkv_weight, qv_bias, out_weight, out_bias, second_gain, expert_norm_bias, up_weight, up_bias, down_weight, down_bias)))
    group_count = TOKENS // (SEQS * S)
    group_rows = SEQS * S
    experts_by_group = row_expert.astype(jnp.int32).reshape(group_count, group_rows)
    keep_by_group = row_keep.astype(jnp.int32).reshape(group_count, group_rows)
    single_by_group = window_resolution.astype(jnp.int32).reshape(group_count, SEQS)
    gathered_source_rows = inputs.astype(jnp.float32).reshape(group_count, group_rows, D)
    checked = jax.checkpoint(block_forward)

    def forward(weights, values):

        def one_group(pieces):
            return checked(weights, pieces[0], pieces[1], pieces[2], pieces[3])
        return lax.map(one_group, (values, experts_by_group, keep_by_group, single_by_group))
    results, pullback = jax.vjp(forward, params, gathered_source_rows)
    grad_params, rowwise_gradient = pullback(cotangent.astype(jnp.float32).reshape(group_count, group_rows, D))
    g_first_gain, g_first_bias, g_qkv, g_qv_bias, g_out_weight, g_out_bias, g_second_gain, g_second_bias, g_up, g_up_bias, g_down, g_down_bias = grad_params
    return (results.reshape(TOKENS, D).astype(jnp.bfloat16), rowwise_gradient.reshape(TOKENS, D).astype(jnp.bfloat16), g_first_gain, g_first_bias, g_qkv, g_qv_bias, g_out_weight, g_out_bias, g_second_gain, g_second_bias, g_up, g_up_bias, g_down, g_down_bias)
```

```python
import math

import jax
import jax.numpy as jnp
from jax import lax
from jax.experimental import pallas as pl
from jax.experimental.pallas import tpu as pltpu
from jax.sharding import PartitionSpec as P

HEAD_DIM = 64
S = 768
TILE = 192
BACK = 672
EPS = 1e-05
MASKED = -1000000000.0
SCALE = 1.0 / math.sqrt(HEAD_DIM)
F32 = jnp.float32
BF16 = jnp.bfloat16

NN = (((1,), (0,)), ((), ()))
NT = (((1,), (1,)), ((), ()))
TN = (((0,), (0,)), ((), ()))


def mm(a, b, dims=NN):
    return lax.dot_general(a, b, dims, preferred_element_type=F32)


def layer_norm(values):
    centred = values - jnp.mean(values, -1, keepdims=True)
    rstd = lax.rsqrt(jnp.mean(centred * centred, -1, keepdims=True) + EPS)
    return centred * rstd, rstd


def norm_back(scaled, xhat, rstd):
    return rstd * (
        scaled
        - jnp.mean(scaled, -1, keepdims=True)
        - xhat * jnp.mean(scaled * xhat, -1, keepdims=True)
    )


def pick_rows(table_ref, expert):
    out = jnp.where(expert == 0, table_ref[0:1, :], table_ref[1:2, :])
    return jnp.where(expert == 2, table_ref[2:3, :], out)


def cost(flops, nbytes, trans=0):
    return pl.CostEstimate(flops=int(flops), bytes_accessed=int(nbytes), transcendentals=int(trans))


def params(**kw):
    return pltpu.CompilerParams(vmem_limit_bytes=56 * 1024 * 1024, **kw)


def attn_fwd_kernel(x_ref, g_ref, b_ref, wt_ref, wb_ref, kb_ref, n1_ref, qkv_ref, mix_ref, lse_ref):
    width = wt_ref.shape[0] // 3
    heads = width // HEAD_DIM
    xhat, _ = layer_norm(x_ref[...].astype(F32))
    normed = (xhat * g_ref[...] + b_ref[...]).astype(BF16)
    n1_ref[...] = normed
    for j in range(3):
        rows = pl.ds(j * width, width)
        part = (mm(wt_ref[rows, :], normed, NT) + wb_ref[rows, :]).astype(BF16)
        if j == 0:
            part = part * jnp.asarray(SCALE, BF16)
        qkv_ref[rows, :] = part
    half = S // 2
    for h in range(heads):
        kt = qkv_ref[pl.ds(width + h * HEAD_DIM, HEAD_DIM), :]
        vt = qkv_ref[pl.ds(2 * width + h * HEAD_DIM, HEAD_DIM), :]
        k = kt.T
        for c in range(2):
            cols = pl.ds(c * half, half)
            qt = qkv_ref[pl.ds(h * HEAD_DIM, HEAD_DIM), cols]
            s = mm(k, qt) + kb_ref[:, c : c + 1]
            top = jnp.max(s, 0, keepdims=True)
            p = jnp.exp(s - top)
            total = jnp.sum(p, 0, keepdims=True)
            o = mm(vt, p.astype(BF16)) * (1.0 / total)
            mix_ref[pl.ds(h * HEAD_DIM, HEAD_DIM), cols] = o.astype(BF16)
            lse_ref[pl.ds(h, 1), cols] = top + jnp.log(total)


def attn_fwd(x, g, b, wt, wb, kb):
    rows, model = x.shape
    width = wt.shape[0] // 3
    heads = width // HEAD_DIM
    return pl.pallas_call(
        attn_fwd_kernel,
        out_shape=(
            jax.ShapeDtypeStruct((rows, model), BF16),
            jax.ShapeDtypeStruct((3 * width, rows), BF16),
            jax.ShapeDtypeStruct((width, rows), BF16),
            jax.ShapeDtypeStruct((heads, rows), F32),
        ),
        compiler_params=params(),
        cost_estimate=cost(2 * rows * model * 3 * width + heads * 8 * rows * rows * 256, 8e6, heads * rows * rows),
        name="attn_fwd",
    )(x, g, b, wt, wb, kb)


def expert_kernel(
    flags_ref, own_ref, pair_ref, far_a_ref, far_b_ref, wo_ref, x_ref, cot_ref, eid_ref,
    ob_ref, g2_ref, b2_ref, ub_ref, up_ref, down_ref,
    mid_ref, n2_ref, act_ref, gpre_ref, out_ref, gn2_ref, small_ref,
    up_v, down_v, xhat_v, gn2_v, sems,
):
    width = own_ref.shape[0]
    experts = up_ref.shape[0]
    up_copy = pltpu.make_async_copy(up_ref, up_v, sems.at[0])
    down_copy = pltpu.make_async_copy(down_ref, down_v, sems.at[1])
    up_copy.start()
    down_copy.start()
    expert = eid_ref[...]
    proj = mm(own_ref[...], wo_ref[0:width, :], TN)
    proj += mm(pair_ref[...], wo_ref[width : 2 * width, :], TN)
    proj += mm(far_a_ref[...] + far_b_ref[...], wo_ref[2 * width :, :], TN)
    middle = x_ref[...].astype(F32) + (proj + ob_ref[...])
    mid_ref[...] = middle
    xhat, _ = layer_norm(middle)
    xhat_v[...] = xhat
    n2_ref[...] = (xhat * pick_rows(g2_ref, expert) + pick_rows(b2_ref, expert)).astype(BF16)
    act_ref[...] = jnp.zeros_like(act_ref)
    gpre_ref[...] = jnp.zeros_like(gpre_ref)
    out_ref[...] = jnp.zeros_like(out_ref)
    gn2_v[...] = jnp.zeros_like(gn2_v)
    small_ref[...] = jnp.zeros_like(small_ref)
    up_copy.wait()
    down_copy.wait()

    def step(i, carry):
        tile, e = i // experts, lax.rem(i, experts)

        @pl.when(flags_ref[i] > 0)
        def _():
            rows = pl.ds(pl.multiple_of(tile * TILE, TILE), TILE)
            mask = (eid_ref[rows, :] == e).astype(F32)
            cot = cot_ref[rows, :]
            pre = mm(n2_ref[rows, :], up_v[e]) + ub_ref[pl.ds(e, 1), :]
            cdf = 0.5 + 0.5 * lax.erf(pre * (1.0 / math.sqrt(2.0)))
            act = (pre * cdf * mask).astype(BF16)
            slope = cdf + pre * (jnp.exp(-0.5 * pre * pre) * (1.0 / math.sqrt(2.0 * math.pi)))
            gpre = (mm(cot, down_v[e], NT) * slope * mask).astype(BF16)
            gn2 = mm(gpre, up_v[e], NT)
            out = mm(act, down_v[e])
            act_ref[rows, :] = act_ref[rows, :] + act
            gpre_ref[rows, :] = gpre_ref[rows, :] + gpre
            out_ref[rows, :] = out_ref[rows, :] + out.astype(BF16)
            gn2_v[rows, :] = gn2_v[rows, :] + gn2.astype(BF16)
            for j, values in enumerate(
                (gn2 * xhat_v[rows, :], gn2, gpre.astype(F32), cot.astype(F32) * mask)
            ):
                at = pl.ds(j * experts + e, 1)
                small_ref[at, :] = small_ref[at, :] + jnp.sum(values, 0, keepdims=True)

        return carry

    lax.fori_loop(0, (S // TILE) * experts, step, 0)
    gn2_ref[...] = gn2_v[0:BACK, :]


def expert_fwd_bwd(flags, own, pair, far_a, far_b, wo, x, cot, eid, ob, g2, b2, ub, up, down):
    rows, model = x.shape
    experts, _, hidden = up.shape
    vmem = pl.BlockSpec(memory_space=pltpu.VMEM)
    hbm = pl.BlockSpec(memory_space=pl.ANY)
    return pl.pallas_call(
        expert_kernel,
        out_shape=(
            jax.ShapeDtypeStruct((rows, model), F32),
            jax.ShapeDtypeStruct((rows, model), BF16),
            jax.ShapeDtypeStruct((rows, hidden), BF16),
            jax.ShapeDtypeStruct((rows, hidden), BF16),
            jax.ShapeDtypeStruct((rows, model), BF16),
            jax.ShapeDtypeStruct((BACK, model), BF16),
            jax.ShapeDtypeStruct((4 * experts, model), F32),
        ),
        in_specs=[pl.BlockSpec(memory_space=pltpu.SMEM)] + [vmem] * 12 + [hbm] * 2,
        out_specs=(vmem,) * 7,
        scratch_shapes=[
            pltpu.VMEM(up.shape, BF16),
            pltpu.VMEM(down.shape, BF16),
            pltpu.VMEM((rows, model), F32),
            pltpu.VMEM((rows, model), BF16),
            pltpu.SemaphoreType.DMA((2,)),
        ],
        compiler_params=params(),
        cost_estimate=cost(2 * rows * model * model + 1.6 * 8 * rows * model * hidden, 22e6, 2 * rows * hidden),
        name="expert_fwd_bwd",
    )(flags, own, pair, far_a, far_b, wo, x, cot, eid, ob, g2, b2, ub, up, down)


def expert_grads_kernel(flags_ref, *refs):
    windows = (len(refs) - 2) // 5
    groups = [refs[5 * w : 5 * w + 5] for w in range(windows)]
    out_ref, acc = refs[-2:]
    experts = pl.num_programs(0)
    e = pl.program_id(0)
    tiles = S // TILE
    model = out_ref.shape[0]
    acc[...] = jnp.zeros_like(acc)
    for w, (n2_ref, act_ref, gpre_ref, cot_ref, eid_ref) in enumerate(groups):

        def step(tile, carry):
            @pl.when(flags_ref[(w * tiles + tile) * experts + e] > 0)
            def _():
                rows = pl.ds(pl.multiple_of(tile * TILE, TILE), TILE)
                mask = (eid_ref[rows, :] == e).astype(BF16)
                acc[:, 0:model] += mm(n2_ref[rows, :], gpre_ref[rows, :] * mask, TN)
                acc[:, model:] += mm(cot_ref[rows, :], act_ref[rows, :] * mask, TN)

            return carry

        lax.fori_loop(0, tiles, step, 0)
    out_ref[...] = acc[...].astype(BF16)


def expert_grads(flags, groups, experts):
    rows, model = groups[0][0].shape
    hidden = groups[0][1].shape[1]
    flat = [a for g in groups for a in g]
    whole = lambda a: pl.BlockSpec(a.shape, lambda e: (0, 0), pipeline_mode=pl.Buffered(1))
    return pl.pallas_call(
        expert_grads_kernel,
        grid=(experts,),
        out_shape=jax.ShapeDtypeStruct((model, experts * 2 * hidden), BF16),
        in_specs=[pl.BlockSpec(memory_space=pltpu.SMEM)] + [whole(a) for a in flat],
        out_specs=pl.BlockSpec((model, 2 * hidden), lambda e: (0, e)),
        scratch_shapes=[pltpu.VMEM((model, 2 * hidden), F32)],
        compiler_params=params(),
        cost_estimate=cost(1.5 * 4 * len(groups) * rows * model * hidden, 22e6),
        name="expert_grads",
    )(flags, *flat)


def mid_back_kernel(s_ref, r_ref, mid_ref, cot_ref, eid_ref, g2_ref, gm_ref, ga_ref):
    total = s_ref[...].astype(F32) + r_ref[...].astype(F32)
    xhat, rstd = layer_norm(mid_ref[...])
    grad = cot_ref[...].astype(F32) + norm_back(total * pick_rows(g2_ref, eid_ref[...]), xhat, rstd)
    gm_ref[...] = grad
    ga_ref[...] = grad.astype(BF16)


def mid_back(s, r, mid, cot, eid, g2):
    model = s.shape[1]
    block = BACK // 3
    row = lambda n: pl.BlockSpec((block, n), lambda i: (i, 0))
    return pl.pallas_call(
        mid_back_kernel,
        grid=(3,),
        out_shape=(jax.ShapeDtypeStruct(s.shape, F32), jax.ShapeDtypeStruct(s.shape, BF16)),
        in_specs=[row(model)] * 4 + [row(1), pl.BlockSpec(g2.shape, lambda i: (0, 0))],
        out_specs=(row(model), row(model)),
        compiler_params=params(),
        cost_estimate=cost(30 * s.size, 16 * s.size),
        name="mid_back",
    )(s, r, mid, cot, eid, g2)


def attn_bwd_kernel(
    flag_ref, ga_ref, far_ref, wo_ref, qkv_ref, mix_ref, lse_ref, kb_ref, wt_ref,
    gaf_ref, dqkv_ref, gn1_ref, gmt_v,
):
    width = wo_ref.shape[0]
    heads = width // HEAD_DIM
    take = flag_ref[0] > 0

    @pl.when(take)
    def _():
        gaf_ref[0:BACK, :] = far_ref[...]

    @pl.when(jnp.logical_not(take))
    def _():
        gaf_ref[0:BACK, :] = ga_ref[...]

    gaf_ref[BACK:, :] = jnp.zeros((S - BACK, gaf_ref.shape[1]), BF16)
    gmt_v[...] = mm(wo_ref[...], gaf_ref[...], NT).astype(BF16)
    half = S // 2
    for h in range(heads):
        at = pl.ds(h * HEAD_DIM, HEAD_DIM)
        kt = qkv_ref[pl.ds(width + h * HEAD_DIM, HEAD_DIM), :]
        vt = qkv_ref[pl.ds(2 * width + h * HEAD_DIM, HEAD_DIM), :]
        k, v = kt.T, vt.T
        dk = dv = None
        for c in range(2):
            cols = pl.ds(c * half, half)
            qt = qkv_ref[at, cols]
            dot = gmt_v[at, cols]
            delta = jnp.sum(dot.astype(F32) * mix_ref[at, cols].astype(F32), 0, keepdims=True)
            s = mm(k, qt) + kb_ref[:, c : c + 1]
            p = jnp.exp(s - lse_ref[pl.ds(h, 1), cols])
            ds = (p * (mm(v, dot) - delta)).astype(BF16)
            dv_c = mm(p.astype(BF16), dot, NT)
            dk_c = mm(ds, qt, NT)
            dv = dv_c if dv is None else dv + dv_c
            dk = dk_c if dk is None else dk + dk_c
            dqkv_ref[at, cols] = (mm(kt, ds) * SCALE).astype(BF16)
        dqkv_ref[pl.ds(width + h * HEAD_DIM, HEAD_DIM), :] = dk.astype(BF16).T
        dqkv_ref[pl.ds(2 * width + h * HEAD_DIM, HEAD_DIM), :] = dv.astype(BF16).T
    gn1_ref[...] = mm(dqkv_ref[:, 0:BACK], wt_ref[...], TN).astype(BF16)


def attn_bwd(flag, ga, far, wo, qkv, mix, lse, kb, wt):
    width, model = wo.shape
    rows = qkv.shape[1]
    heads = width // HEAD_DIM
    vmem = pl.BlockSpec(memory_space=pltpu.VMEM)
    return pl.pallas_call(
        attn_bwd_kernel,
        out_shape=(
            jax.ShapeDtypeStruct((rows, model), BF16),
            jax.ShapeDtypeStruct(qkv.shape, BF16),
            jax.ShapeDtypeStruct((BACK, model), BF16),
        ),
        in_specs=[pl.BlockSpec(memory_space=pltpu.SMEM)] + [vmem] * 8,
        out_specs=(vmem,) * 3,
        scratch_shapes=[pltpu.VMEM((width, rows), BF16)],
        compiler_params=params(),
        cost_estimate=cost(2 * rows * model * 4 * width + heads * 16 * rows * rows * 256, 9e6, heads * rows * rows),
        name="attn_bwd",
    )(flag, ga, far, wo, qkv, mix, lse, kb, wt)


def attn_grads_kernel(*refs):
    windows = (len(refs) - 4) // 6
    groups = [refs[6 * w : 6 * w + 6] for w in range(windows)]
    out_ref, rows_ref, cols_ref, acc = refs[-4:]
    wide = groups[0][1].shape[0]
    rows_ref[...] = jnp.zeros_like(rows_ref)
    cols = None
    for w, (n1_ref, dqkv_ref, mix_ref, gaf_ref, x_ref, gn1_ref) in enumerate(groups):
        qkv_part = mm(dqkv_ref[...], n1_ref[...])
        out_part = mm(mix_ref[...], gaf_ref[...])
        if w == 0:
            acc[0:wide, :] = qkv_part
            acc[wide:, :] = out_part
        else:
            acc[0:wide, :] += qkv_part
            acc[wide:, :] += out_part
        col = jnp.sum(dqkv_ref[...].astype(F32), 1, keepdims=True)
        cols = col if cols is None else cols + col
        xhat, _ = layer_norm(x_ref[0:BACK, :].astype(F32))
        grad = gn1_ref[...].astype(F32)
        for j, values in enumerate((grad * xhat, grad, gaf_ref[...].astype(F32))):
            rows_ref[j : j + 1, :] = rows_ref[j : j + 1, :] + jnp.sum(values, 0, keepdims=True)
    cols_ref[...] = cols
    out_ref[...] = acc[...].astype(BF16).T


def attn_grads(groups):
    n1, dqkv, mix = groups[0][:3]
    wide = dqkv.shape[0] + mix.shape[0]
    model = n1.shape[1]
    flat = [a for g in groups for a in g]
    return pl.pallas_call(
        attn_grads_kernel,
        out_shape=(
            jax.ShapeDtypeStruct((model, wide), BF16),
            jax.ShapeDtypeStruct((8, model), F32),
            jax.ShapeDtypeStruct((dqkv.shape[0], 1), F32),
        ),
        scratch_shapes=[pltpu.VMEM((wide, model), F32)],
        compiler_params=params(),
        cost_estimate=cost(len(groups) * 2 * n1.shape[0] * model * wide, 18e6),
        name="attn_grads",
    )(*flat)


def first_back_kernel(s_ref, r_ref, gm_ref, x_ref, g_ref, out_ref):
    total = s_ref[...].astype(F32) + r_ref[...].astype(F32)
    xhat, rstd = layer_norm(x_ref[...].astype(F32))
    out_ref[...] = (gm_ref[...] + norm_back(total * g_ref[...], xhat, rstd)).astype(BF16)


def first_back(s, r, gm, x, g):
    model = s.shape[1]
    block = BACK // 3
    row = lambda n: pl.BlockSpec((block, n), lambda i: (i, 0))
    return pl.pallas_call(
        first_back_kernel,
        grid=(3,),
        out_shape=jax.ShapeDtypeStruct(s.shape, BF16),
        in_specs=[row(model)] * 4 + [pl.BlockSpec(g.shape, lambda i: (0, 0))],
        out_specs=row(model),
        compiler_params=params(),
        cost_estimate=cost(30 * s.size, 12 * s.size),
        name="first_back",
    )(s, r, gm, x, g)


def layer_out_kernel(s_ref, r_ref, mid_ref, eid_ref, db_ref, out_ref):
    total = s_ref[...].astype(F32) + r_ref[...].astype(F32)
    out_ref[...] = (mid_ref[...] + (total + pick_rows(db_ref, eid_ref[...]))).astype(BF16)


def layer_out_rows(s, r, mid, eid, db):
    rows, model = s.shape
    row = lambda n: pl.BlockSpec((TILE, n), lambda i: (i, 0))
    return pl.pallas_call(
        layer_out_kernel,
        grid=(rows // TILE,),
        out_shape=jax.ShapeDtypeStruct(s.shape, BF16),
        in_specs=[row(model)] * 3 + [row(1), pl.BlockSpec(db.shape, lambda i: (0, 0))],
        out_specs=row(model),
        compiler_params=params(),
        cost_estimate=cost(5 * s.size, 10 * s.size),
        name="layer_out_rows",
    )(s, r, mid, eid, db)


def inward(v):
    return lax.ppermute(v, "tensor", [(0, 1), (3, 2)])


def across(v):
    return lax.ppermute(v, "tensor", [(1, 2), (2, 1)])


def outward(v):
    return lax.ppermute(v, "tensor", [(1, 0), (2, 3)])


def pairs(v):
    return lax.ppermute(v, "tensor", [(0, 1), (1, 0), (2, 3), (3, 2)])


def add_rounded(a, b):
    return (a.astype(F32) + b.astype(F32)).astype(BF16)


def body(
    inputs, cotangent, row_expert, row_keep, window_resolution, attention_norm_gain,
    attention_norm_bias, qkv_weight, qv_bias, out_weight, out_bias, second_gain,
    expert_norm_bias, up_weight, up_bias, down_weight, down_bias,
):
    row_count, model = inputs.shape
    experts = up_weight.shape[0]
    width = qkv_weight.shape[2]
    windows = row_count // S
    tiles = S // TILE
    me = lax.axis_index("tensor")
    at_end = (me == 0) | (me == 3)
    end_flag = at_end.astype(jnp.int32).reshape(1)

    wt = jnp.transpose(qkv_weight, (0, 2, 1)).reshape(3 * width, model)
    bias_pair = qv_bias.reshape(2, width)
    wb = jnp.concatenate([bias_pair[0], jnp.zeros((width,), F32), bias_pair[1]]).reshape(3 * width, 1)
    keep = row_keep.reshape(windows, S) > 0
    single = window_resolution.reshape(windows, 1) > 0
    upper = (jnp.arange(S) >= S // 2)[None, :]
    kb = jnp.stack([keep & (single | ~upper), keep & (single | upper)], -1)
    kb = jnp.where(kb, 0.0, MASKED).astype(F32)
    eid = row_expert.reshape(windows, S, 1)
    onehot = row_expert.reshape(windows, tiles, TILE, 1) == jnp.arange(experts)
    flags = jnp.any(onehot, 2).astype(jnp.int32).reshape(windows, tiles * experts)
    real = onehot & (row_keep.reshape(windows, tiles, TILE, 1) > 0)
    back_flags = jnp.any(real, 2).astype(jnp.int32).reshape(-1)
    g1, b1 = attention_norm_gain.reshape(1, model), attention_norm_bias.reshape(1, model)
    ob = out_bias.reshape(1, model)

    shards = lax.all_gather(out_weight, "tensor", axis=0)
    near = me ^ 1
    far = jnp.where(me < 2, 2, 1)
    order = jnp.stack([me, near, far, jnp.where(me < 2, 3, 0)])
    wo_all = shards[order].reshape(model, model)

    xs = [inputs[w * S : (w + 1) * S] for w in range(windows)]
    cots = [cotangent[w * S : (w + 1) * S] for w in range(windows)]

    fwd = [attn_fwd(xs[w], g1, b1, wt, wb, kb[w]) for w in range(windows)]
    ex = []
    for w in range(windows):
        own = fwd[w][2]
        pair = pairs(own)
        far_a = across(jnp.concatenate([own, pair], 0))
        far_b = outward(far_a)
        ex.append(
            expert_fwd_bwd(
                flags[w], own, pair, far_a, far_b, wo_all, xs[w], cots[w], eid[w],
                ob, second_gain, expert_norm_bias, up_bias, up_weight, down_weight,
            )
        )
    mids = []
    for w in range(windows):
        mid, gn2 = ex[w][0], ex[w][5]
        s = add_rounded(gn2, inward(gn2))
        mids.append(mid_back(s, across(s), mid[:BACK], cots[w][:BACK], eid[w][:BACK], second_gain))
    bwd = []
    for w in range(windows):
        n1, qkv, mix, lse = fwd[w]
        ga = mids[w][1]
        bwd.append(attn_bwd(end_flag, ga, outward(ga), out_weight, qkv, mix, lse, kb[w], wt))
    rows_grad = []
    for w in range(windows):
        gn1 = bwd[w][2]
        s = add_rounded(gn1, inward(gn1))
        grad = first_back(s, across(s), mids[w][0], xs[w][:BACK], g1)
        grad = jnp.where(at_end, outward(grad), grad)
        rows_grad.append(jnp.concatenate([grad, jnp.zeros((S - BACK, model), BF16)], 0))
    outs = []
    for w in range(windows):
        part = ex[w][4]
        s = add_rounded(part, inward(part))
        rows_out = layer_out_rows(s, across(s), ex[w][0], eid[w], down_bias)
        outs.append(jnp.where(at_end, outward(rows_out), rows_out))

    groups = [(ex[w][1], ex[w][2], ex[w][3], cots[w], eid[w]) for w in range(windows)]
    expert_g = expert_grads(back_flags, groups, experts)
    expert_g = lax.psum_scatter(expert_g, "dp", scatter_dimension=0, tiled=True).astype(F32)
    groups = [(fwd[w][0], bwd[w][1], fwd[w][2], bwd[w][0], xs[w], bwd[w][2]) for w in range(windows)]
    attn_g, row_sums, col_sums = attn_grads(groups)
    attn_g = lax.psum_scatter(attn_g, "dp", scatter_dimension=0, tiled=True).astype(F32)

    shared = jnp.where(me == 0, 1.0, 0.0)
    small = sum(ex[w][6] for w in range(windows))
    whole = jnp.concatenate(
        [
            small[: 2 * experts],
            small[3 * experts :] * shared,
            row_sums[0:2],
            row_sums[2:3] * shared,
        ],
        0,
    )
    whole = lax.psum(whole, ("dp", "tensor"))
    local = lax.psum(
        jnp.concatenate([small[2 * experts : 3 * experts].reshape(-1), col_sums.reshape(-1)]), "dp"
    )
    block = expert_g.shape[0]
    hidden = up_weight.shape[2]
    expert_g = expert_g.reshape(block, experts, 2, hidden)
    grad_up = jnp.transpose(expert_g[:, :, 0], (1, 0, 2))
    grad_down = jnp.transpose(expert_g[:, :, 1], (1, 2, 0))
    grad_qkv = jnp.transpose(attn_g[:, : 3 * width].reshape(block, 3, width), (1, 0, 2))
    grad_out = attn_g[:, 3 * width :].T
    up_bias_grad = local[: experts * hidden].reshape(experts, hidden)
    cols = local[experts * hidden :].reshape(3, width)
    qv_grad = jnp.stack([cols[0], cols[2]]).reshape(qv_bias.shape)
    return (
        jnp.concatenate(outs, 0),
        jnp.concatenate(rows_grad, 0),
        whole[3 * experts],
        whole[3 * experts + 1],
        grad_qkv,
        qv_grad,
        grad_out,
        whole[3 * experts + 2],
        whole[:experts],
        whole[experts : 2 * experts],
        grad_up,
        up_bias_grad,
        grad_down,
        whole[2 * experts : 3 * experts],
    )


def solution(mesh):
    in_specs = (
        P("dp", None), P("dp", None), P("dp"), P("dp"), P("dp"), P(), P(),
        P(None, None, "tensor"), P(None, "tensor", None), P("tensor", None), P(), P(), P(),
        P(None, None, "tensor"), P(None, "tensor"), P(None, "tensor", None), P(),
    )
    out_specs = (
        P("dp", None), P("dp", None), P(), P(), P(None, "dp", "tensor"), P(None, "tensor", None),
        P("tensor", "dp"), P(), P(), P(), P(None, "dp", "tensor"), P(None, "tensor"),
        P(None, "tensor", "dp"), P(),
    )
    return jax.shard_map(body, mesh=mesh, in_specs=in_specs, out_specs=out_specs, check_vma=False)
```

```python
import functools
import math

import jax
import jax.numpy as jnp
from jax import lax
from jax.experimental import pallas as pl
from jax.experimental.pallas import tpu as pltpu
from jax.sharding import PartitionSpec as P

HEAD_DIM = 64
S = 768
TILE = 192
BACK = 672
EXPERT_MIB = 32
GRADS_MIB = 20
EPS = 1e-05
MASKED = -1000000000.0
SCALE = 1.0 / math.sqrt(HEAD_DIM)
F32 = jnp.float32
BF16 = jnp.bfloat16

NN = (((1,), (0,)), ((), ()))
NT = (((1,), (1,)), ((), ()))
TN = (((0,), (0,)), ((), ()))


def mm(a, b, dims=NN):
    return lax.dot_general(a, b, dims, preferred_element_type=F32)


def row_mean(v):
    lanes = 128
    total = v[:, 0:lanes]
    for i in range(1, v.shape[1] // lanes):
        total = total + v[:, i * lanes : (i + 1) * lanes]
    return jnp.sum(total, -1, keepdims=True) * (1.0 / v.shape[1])


def layer_norm(values):
    centred = values - row_mean(values)
    rstd = lax.rsqrt(row_mean(centred * centred) + EPS)
    return centred * rstd, rstd


def norm_back(scaled, xhat, rstd):
    return rstd * (scaled - row_mean(scaled) - xhat * row_mean(scaled * xhat))


def pick_rows(table_ref, expert):
    out = jnp.where(expert == 0, table_ref[0:1, :], table_ref[1:2, :])
    return jnp.where(expert == 2, table_ref[2:3, :], out)


def cost(*_):
    return pl.CostEstimate(flops=int(1e11), bytes_accessed=1, transcendentals=0)


def window(w, n, rows=S):
    return pl.BlockSpec((rows, n), lambda i: (w, 0))


def full(a):
    return pl.BlockSpec(a.shape, lambda i: (0,) * a.ndim)


def params(mib):
    return pltpu.CompilerParams(vmem_limit_bytes=mib * 1024 * 1024)


def heads_forward(qkv_ref, cols_ref, mix_ref, lse_ref, base):
    width = qkv_ref.shape[0] // 3
    first = base // HEAD_DIM
    half = S // 2
    for h in range(width // HEAD_DIM):
        kt = qkv_ref[pl.ds(width + h * HEAD_DIM, HEAD_DIM), :]
        vt = qkv_ref[pl.ds(2 * width + h * HEAD_DIM, HEAD_DIM), :]
        k = kt.T
        for c in range(2):
            at = pl.ds(c * half, half)
            qt = qkv_ref[pl.ds(h * HEAD_DIM, HEAD_DIM), at]
            s = mm(k, qt) + cols_ref[:, c + 1 : c + 2]
            top = jnp.max(s, 0, keepdims=True)
            p = jnp.exp(s - top)
            total = jnp.sum(p, 0, keepdims=True)
            o = mm(vt, p.astype(BF16)) * (1.0 / total)
            mix_ref[pl.ds(base + h * HEAD_DIM, HEAD_DIM), at] = o.astype(BF16)
            lse_ref[pl.ds(first + h, 1), at] = top + jnp.log(total)


def project(wt_ref, wb_ref, normed, qkv_ref):
    width = wt_ref.shape[0] // 3
    bias = wb_ref[...].T
    for j in range(3):
        rows = pl.ds(j * width, width)
        shift = bias[j * width : (j + 1) * width, 0:1]
        part = (mm(wt_ref[rows, :], normed, NT) + shift).astype(BF16)
        if j == 0:
            part = part * jnp.asarray(SCALE, BF16)
        qkv_ref[rows, :] = part


HBM = pl.BlockSpec(memory_space=pltpu.HBM)
SMEM = pl.BlockSpec(memory_space=pltpu.SMEM)
VMEM = pl.BlockSpec(memory_space=pltpu.VMEM)


def start(source, target, sem):
    copy = pltpu.make_async_copy(source, target, sem)
    copy.start()
    return copy


def attn_own_kernel(
    x_ref, rows_ref, g_ref, b_ref, wt_ref, wb_ref, lse_ref, n1_ref, qkv_ref, mix_ref, cols_ref
):
    cols_ref[...] = rows_ref[...].T
    xhat, _ = layer_norm(x_ref[...].astype(F32))
    n1_ref[...] = (xhat * g_ref[...] + b_ref[...]).astype(BF16)
    project(wt_ref, wb_ref, n1_ref[...], qkv_ref)
    heads_forward(qkv_ref, cols_ref, mix_ref, lse_ref, 0)


def attn_own(x, facts, g, b, wt, wb):
    rows, model = x.shape
    width = wt.shape[0] // 3
    return pl.pallas_call(
        attn_own_kernel,
        out_shape=(
            jax.ShapeDtypeStruct((width // HEAD_DIM, rows), F32),
            jax.ShapeDtypeStruct((rows, model), BF16),
            jax.ShapeDtypeStruct((3 * width, rows), BF16),
            jax.ShapeDtypeStruct((width, rows), BF16),
            jax.ShapeDtypeStruct((rows, facts.shape[0]), F32),
        ),
        in_specs=[VMEM] * 6,
        out_specs=(VMEM,) * 5,
        compiler_params=params(14),
        cost_estimate=cost(),
        name="attn_own",
    )(x, facts, g, b, wt, wb)


def attn_comp_kernel(
    emit, role_ref, near_ref, far_ref, wt_ref, wo_ref, n1_ref, own_qkv_ref, own_ref, own_lse_ref, cols_ref, wb_ref,
    lse_ref, qkv_ref, mix_ref, *refs
):
    width = own_ref.shape[0]
    wide = 3 * width
    heads = width // HEAD_DIM
    if emit:
        wt_c_ref, wt_both_ref, wo_both_ref, wo_c_ref, pack_v = refs
        for j in range(4):
            at = pl.ds(pl.multiple_of(role_ref[7 + j] * width, width), width)
            pack_v[at, :] = (near_ref, far_ref)[j // 2][(j % 2) * width : (j % 2 + 1) * width, :]
        wt_c_ref[...] = pack_v[0:wide, :]
        wo_both_ref[0:width, :] = wo_ref[...]
        wo_both_ref[width:, :] = pack_v[wide:, :]
        wo_c_ref[...] = pack_v[wide:, :]
        wt_both_ref[pl.ds(pl.multiple_of(role_ref[1] * wide, wide), wide), :] = wt_ref[...]
        wt_both_ref[pl.ds(pl.multiple_of(role_ref[2] * wide, wide), wide), :] = pack_v[0:wide, :]
        weights = wt_c_ref
    else:
        weights = wt_ref
    qkv_ref[0:wide, :] = own_qkv_ref[...]
    mix_ref[0:width, :] = own_ref[...]
    lse_ref[0:heads, :] = own_lse_ref[...]
    comp = qkv_ref.at[pl.ds(wide, wide), :]
    project(weights, wb_ref, n1_ref[...], comp)
    heads_forward(comp, cols_ref, mix_ref, lse_ref, width)


def attn_comp(emit, role, near, far, wt, wo, own, cols, wb):
    own_lse, n1, own_qkv, own_mix = own[:4]
    rows, model = n1.shape
    width = own_mix.shape[0]
    outs = [
        jax.ShapeDtypeStruct((2 * (width // HEAD_DIM), rows), F32),
        jax.ShapeDtypeStruct((6 * width, rows), BF16),
        jax.ShapeDtypeStruct((2 * width, rows), BF16),
    ]
    if emit:
        outs += [
            jax.ShapeDtypeStruct((3 * width, model), BF16),
            jax.ShapeDtypeStruct((6 * width, model), BF16),
            jax.ShapeDtypeStruct((2 * width, model), BF16),
            jax.ShapeDtypeStruct((width, model), BF16),
        ]
    given = (near, far, wt, wo) if emit else (wt,)
    kernel = functools.partial(attn_comp_kernel, True) if emit else attn_comp_later
    return pl.pallas_call(
        kernel,
        out_shape=tuple(outs),
        in_specs=[SMEM] + [VMEM] * (len(given) + 6),
        out_specs=(VMEM,) * len(outs),
        scratch_shapes=[pltpu.VMEM((4 * width, model), BF16)] if emit else [],
        compiler_params=params(18 if emit else 14),
        cost_estimate=cost(),
        name="attn_comp",
    )(role, *given, n1, own_qkv, own_mix, own_lse, cols, wb)


def attn_comp_later(role_ref, wt_ref, *refs):
    attn_comp_kernel(False, role_ref, None, None, wt_ref, None, *refs)


def present(first_ref, res_ref, w, tile, e):
    single = res_ref[w] > 0
    second = jnp.logical_and(jnp.logical_not(single), tile >= (S // TILE) // 2)
    image = first_ref[2 * w + second.astype(jnp.int32)]
    mixed = tile == S // TILE - 1
    mixed = jnp.logical_or(mixed, jnp.logical_and(jnp.logical_not(single), tile == (S // TILE) // 2 - 1))
    return jnp.logical_or(e == image, jnp.logical_and(mixed, e == 1))


def expert_kernel(
    w, role_ref, first_ref, res_ref, mix_ref, far_ref, wo_ref, wo_far_ref, wo_far_comp_ref, x_ref, cot_v,
    cols_ref, ob_ref, g2_ref, b2_ref, ub_ref, up_v, down_v,
    small_ref, mid_ref, n2_v, act_v, gpre_v, out_v, gn2_ref,
    mix_v, wo_v, xhat_v, gn2_v,
):
    experts = up_v.shape[0]
    width = mix_ref.shape[0] // 2
    tiles = S // TILE
    for j in range(4):
        at = pl.ds(pl.multiple_of(role_ref[3 + j] * width, width), width)
        piece = slice((j % 2) * width, (j % 2 + 1) * width)
        mix_v[at, :] = (mix_ref, far_ref)[j // 2][piece, :]
        wo_v[at, :] = wo_ref[piece, :] if j < 2 else (wo_far_ref, wo_far_comp_ref)[j - 2][...]
    expert = cols_ref[:, 0:1]
    small_ref[...] = jnp.zeros_like(small_ref)
    proj = mm(mix_v[...], wo_v[...], TN)
    middle = x_ref[...].astype(F32) + (proj + ob_ref[...])
    mid_ref[...] = middle.astype(BF16)
    xhat, _ = layer_norm(middle)
    xhat_v[...] = xhat
    n2_v[...] = (xhat * pick_rows(g2_ref, expert) + pick_rows(b2_ref, expert)).astype(BF16)

    def tile_step(tile, carry):
        at = pl.ds(pl.multiple_of(tile * TILE, TILE), TILE)
        for ref in (act_v, gpre_v, out_v, gn2_v):
            ref[at, :] = jnp.zeros((TILE, ref.shape[1]), BF16)

        def step(e, carry):
            @pl.when(present(first_ref, res_ref, w, tile, e))
            def _():
                mask = (cols_ref[at, 0:1] == e.astype(F32)).astype(F32)
                cot = cot_v[at, :]
                pre = mm(n2_v[at, :], up_v[e]) + ub_ref[pl.ds(e, 1), :]
                cdf = 0.5 + 0.5 * lax.erf(pre * (1.0 / math.sqrt(2.0)))
                act = (pre * cdf * mask).astype(BF16)
                slope = cdf + pre * (jnp.exp(-0.5 * pre * pre) * (1.0 / math.sqrt(2.0 * math.pi)))
                gpre = (mm(cot, down_v[e], NT) * slope * mask).astype(BF16)
                gn2 = mm(gpre, up_v[e], NT)
                out = mm(act, down_v[e])
                act_v[at, :] = act_v[at, :] + act
                gpre_v[at, :] = gpre_v[at, :] + gpre
                out_v[at, :] = out_v[at, :] + out.astype(BF16)
                gn2_v[at, :] = gn2_v[at, :] + gn2.astype(BF16)
                for j, values in enumerate(
                    (gn2 * xhat_v[at, :], gn2, gpre.astype(F32), cot.astype(F32) * mask)
                ):
                    row = pl.ds(j * experts + e, 1)
                    small_ref[row, :] = small_ref[row, :] + jnp.sum(values, 0, keepdims=True)

            return carry

        lax.fori_loop(0, experts, step, 0)
        return carry

    lax.fori_loop(0, tiles, tile_step, 0)
    gn2_ref[...] = gn2_v[0:BACK, :]


def expert_fwd_bwd(w, role, first, res, mix, far, wo, x, cot, cols, ob, g2, b2, ub, up, down):
    rows, model = x.shape
    experts, _, hidden = up.shape
    return pl.pallas_call(
        functools.partial(expert_kernel, w),
        out_shape=(
            jax.ShapeDtypeStruct((4 * experts, model), F32),
            jax.ShapeDtypeStruct((rows, model), BF16),
            jax.ShapeDtypeStruct((rows, model), BF16),
            jax.ShapeDtypeStruct((rows, hidden), BF16),
            jax.ShapeDtypeStruct((rows, hidden), BF16),
            jax.ShapeDtypeStruct((rows, model), BF16),
            jax.ShapeDtypeStruct((BACK, model), BF16),
        ),
        in_specs=[SMEM] * 3 + [VMEM] * 14,
        out_specs=(VMEM,) * 7,
        scratch_shapes=[
            pltpu.VMEM((rows, model), BF16),
            pltpu.VMEM((rows, model), BF16),
            pltpu.VMEM((rows, model), F32),
            pltpu.VMEM((rows, model), BF16),
        ],
        compiler_params=params(EXPERT_MIB),
        cost_estimate=cost(),
        name="expert_fwd_bwd",
    )(role, first, res, mix, far, *wo, x, cot, cols, ob, g2, b2, ub, up, down)


def expert_grads_kernel(windows, first_ref, res_ref, *refs):
    groups = [refs[5 * w : 5 * w + 5] for w in range(windows)]
    out_ref, acc = refs[-2:]
    e, kind = pl.program_id(0), pl.program_id(1)
    tiles = S // TILE
    acc[...] = jnp.zeros_like(acc)

    def add(cols_ref, row, count, left, right):
        at = pl.ds(pl.multiple_of(row, TILE), count)
        mask = (cols_ref[at, 0:1] == e.astype(F32)).astype(BF16)
        acc[...] += mm(left[at, :], right[at, :] * mask, TN)

    def half_step(w, half, carry):
        n2_ref, act_ref, gpre_ref, cot_ref, cols_ref = groups[w]
        tile = 2 * half
        row = tile * TILE
        here = present(first_ref, res_ref, w, tile, e)
        next_ = present(first_ref, res_ref, w, tile + 1, e)
        for k, (left, right) in enumerate(((n2_ref, gpre_ref), (cot_ref, act_ref))):

            @pl.when(jnp.logical_and(kind == k, jnp.logical_and(here, next_)))
            def _():
                add(cols_ref, row, 2 * TILE, left, right)

            @pl.when(jnp.logical_and(kind == k, here != next_))
            def _():
                add(cols_ref, row + jnp.where(here, 0, TILE), TILE, left, right)

        return carry

    for w in range(windows):
        lax.fori_loop(0, tiles // 2, functools.partial(half_step, w), 0)
    out_ref[...] = acc[...].astype(BF16)


def expert_grads(first, res, groups, experts):
    model = groups[0][0].shape[1]
    hidden = groups[0][1].shape[1]
    flat = [a for g in groups for a in g]
    return pl.pallas_call(
        functools.partial(expert_grads_kernel, len(groups)),
        grid=(experts, 2),
        out_shape=jax.ShapeDtypeStruct((model, 2 * experts * hidden), BF16),
        in_specs=[SMEM] * 2 + [VMEM] * len(flat),
        out_specs=pl.BlockSpec((model, hidden), lambda e, k: (0, k * experts + e)),
        scratch_shapes=[pltpu.VMEM((model, hidden), F32)],
        compiler_params=params(GRADS_MIB),
        cost_estimate=cost(),
        name="expert_grads",
    )(first, res, *flat)


def mid_back_kernel(s_ref, r_ref, mid_ref, cot_ref, cols_ref, g2_ref, ga_ref):
    top = slice(0, BACK)
    total = s_ref[...].astype(F32) + r_ref[...].astype(F32)
    xhat, rstd = layer_norm(mid_ref[top, :].astype(F32))
    gain = pick_rows(g2_ref, cols_ref[top, 0:1])
    grad = cot_ref[top, :].astype(F32) + norm_back(total * gain, xhat, rstd)
    ga_ref[...] = grad.astype(BF16)


def mid_back(s, r, mid, cot, cols, g2):
    return pl.pallas_call(
        mid_back_kernel,
        out_shape=jax.ShapeDtypeStruct(s.shape, BF16),
        in_specs=[VMEM] * 6,
        out_specs=VMEM,
        compiler_params=params(16),
        cost_estimate=cost(),
        name="mid_back",
    )(s, r, mid, cot, cols, g2)


def attn_bwd_kernel(
    role_ref, ga_ref, far_ref, cols_ref, wt_ref, wo_ref, mix_ref, qkv_ref, lse_ref,
    gn1_ref, dqkv_ref, gaf_ref, gmt_v,
):
    width = wo_ref.shape[0] // 2
    wide = 3 * width
    heads = width // HEAD_DIM
    take = role_ref[0] > 0
    top = pl.ds(0, BACK)

    @pl.when(take)
    def _():
        gaf_ref[top, :] = far_ref[...]

    @pl.when(jnp.logical_not(take))
    def _():
        gaf_ref[top, :] = ga_ref[...]

    gaf_ref[BACK:, :] = jnp.zeros((S - BACK, gaf_ref.shape[1]), BF16)
    gmt_v[...] = mm(wo_ref[...], gaf_ref[...], NT).astype(BF16)
    half = S // 2

    def group(g, carry):
        into = role_ref[1 + g] * wide
        for h in range(heads):
            at = lambda base, step: pl.ds(pl.multiple_of(base + h * HEAD_DIM, HEAD_DIM), HEAD_DIM)
            both = at(g * width, 0)
            q_rows, k_rows, v_rows = (at(g * wide + j * width, 0) for j in range(3))
            q_into, k_into, v_into = (at(into + j * width, 0) for j in range(3))
            kt, vt = qkv_ref[k_rows, :], qkv_ref[v_rows, :]
            k, v = kt.T, vt.T
            row = pl.ds(g * heads + h, 1)
            dk = dv = None
            for c in range(2):
                part = pl.ds(c * half, half)
                qt = qkv_ref[q_rows, part]
                dot = gmt_v[both, part]
                delta = jnp.sum(dot.astype(F32) * mix_ref[both, part].astype(F32), 0, keepdims=True)
                s = mm(k, qt) + cols_ref[:, c + 1 : c + 2]
                p = jnp.exp(s - lse_ref[row, part])
                ds = (p * (mm(v, dot) - delta)).astype(BF16)
                dv_c = mm(p.astype(BF16), dot, NT)
                dk_c = mm(ds, qt, NT)
                dv = dv_c if dv is None else dv + dv_c
                dk = dk_c if dk is None else dk + dk_c
                dqkv_ref[q_into, part] = (mm(kt, ds) * SCALE).astype(BF16)
            dqkv_ref[k_into, :] = dk.astype(BF16).T
            dqkv_ref[v_into, :] = dv.astype(BF16).T
        return carry

    lax.fori_loop(0, 2, group, 0)
    gn1_ref[...] = mm(dqkv_ref[:, 0:BACK], wt_ref[...], TN).astype(BF16)


def attn_bwd(role, ga, far, cols, wt, wo, mix, qkv, lse):
    model = wo.shape[1]
    return pl.pallas_call(
        attn_bwd_kernel,
        out_shape=(
            jax.ShapeDtypeStruct((BACK, model), BF16),
            jax.ShapeDtypeStruct(qkv.shape, BF16),
            jax.ShapeDtypeStruct((S, model), BF16),
        ),
        in_specs=[SMEM] + [VMEM] * 8,
        out_specs=(VMEM,) * 3,
        scratch_shapes=[pltpu.VMEM(mix.shape, BF16)],
        compiler_params=params(20),
        cost_estimate=cost(),
        name="attn_bwd",
    )(role, ga, far, cols, wt, wo, mix, qkv, lse)


def attn_grads_kernel(role_ref, *refs):
    windows = (len(refs) - 8) // 4
    groups = [refs[4 * w : 4 * w + 4] for w in range(windows)]
    out_ref, sum_ref, n1_v, gaf_v, dqkv_v, mix_v, acc, sems = refs[-8:]
    wide = dqkv_v.shape[0]
    own = pl.ds(pl.multiple_of(role_ref[1] * wide, wide), wide)
    loads = []
    for w, (n1_ref, dqkv_ref, mix_ref, gaf_ref) in enumerate(groups):
        at = pl.ds(w * S, S)
        pairs = (
            (dqkv_ref.at[own, :], dqkv_v.at[:, at]),
            (n1_ref, n1_v.at[at, :]),
            (mix_ref, mix_v.at[:, at]),
            (gaf_ref, gaf_v.at[at, :]),
        )
        loads += [start(a, b, sems.at[4 * w + j]) for j, (a, b) in enumerate(pairs)]
    for load in loads:
        load.wait()
    acc[0:wide, :] = mm(dqkv_v[...], n1_v[...])
    acc[wide:, :] = mm(mix_v[...], gaf_v[...])
    sum_ref[...] = mm(jnp.ones((8, dqkv_v.shape[1]), BF16), dqkv_v[...], NT)
    out_ref[...] = acc[...].astype(BF16).T


def attn_grads(role, groups):
    n1, dqkv, mix = groups[0][:3]
    model = n1.shape[1]
    wide = dqkv.shape[0] // 2
    rows = len(groups) * S
    flat = [a for g in groups for a in g]
    outs = (
        jax.ShapeDtypeStruct((model, wide + mix.shape[0]), BF16),
        jax.ShapeDtypeStruct((8, wide), F32),
    )
    return pl.pallas_call(
        attn_grads_kernel,
        grid=(1,),
        out_shape=outs,
        in_specs=[SMEM] + [HBM] * len(flat),
        out_specs=tuple(full(o) for o in outs),
        scratch_shapes=[
            pltpu.VMEM((rows, model), BF16),
            pltpu.VMEM((rows, model), BF16),
            pltpu.VMEM((wide, rows), BF16),
            pltpu.VMEM((mix.shape[0], rows), BF16),
            pltpu.VMEM((wide + mix.shape[0], model), F32),
            pltpu.SemaphoreType.DMA((4 * len(groups),)),
        ],
        compiler_params=params(26),
        cost_estimate=cost(),
        name="attn_grads",
    )(role, *flat)


def first_back_kernel(s_ref, r_ref, ga_ref, x_ref, g_ref, *refs):
    out_ref, sum_ref = refs[-2:]
    top = slice(0, BACK)
    total = s_ref[...].astype(F32) + r_ref[...].astype(F32)
    xhat, rstd = layer_norm(x_ref[top, :].astype(F32))
    ga = ga_ref[top, :].astype(F32)
    sum_ref[...] = jnp.zeros_like(sum_ref)
    for j, values in enumerate((total * xhat, total, ga)):
        sum_ref[j : j + 1, :] = jnp.sum(values, 0, keepdims=True)
    back = norm_back(total * g_ref[...], xhat, rstd)
    out_ref[top, :] = (ga + back).astype(BF16)
    out_ref[BACK:, :] = jnp.zeros((S - BACK, out_ref.shape[1]), BF16)


def first_back(s, r, ga, x, g):
    model = s.shape[1]
    return pl.pallas_call(
        first_back_kernel,
        out_shape=(
            jax.ShapeDtypeStruct(x.shape, BF16),
            jax.ShapeDtypeStruct((8, model), F32),
        ),
        in_specs=[VMEM] * 5,
        out_specs=(VMEM, VMEM),
        compiler_params=params(16),
        cost_estimate=cost(),
        name="first_back",
    )(s, r, ga, x, g)


def layer_out_kernel(s_ref, r_ref, mid_ref, cols_ref, db_ref, out_ref):
    total = s_ref[...].astype(F32) + r_ref[...].astype(F32)
    shift = pick_rows(db_ref, cols_ref[:, 0:1])
    out_ref[...] = (mid_ref[...].astype(F32) + (total + shift)).astype(BF16)


def layer_out_rows(s, r, mid, cols, db):
    return pl.pallas_call(
        layer_out_kernel,
        out_shape=jax.ShapeDtypeStruct(mid.shape, BF16),
        in_specs=[VMEM] * 5,
        out_specs=VMEM,
        compiler_params=params(16),
        cost_estimate=cost(),
        name="layer_out_rows",
    )(s, r, mid, cols, db)


def inward(v):
    return lax.ppermute(v, "tensor", [(0, 1), (3, 2)])


def across(v):
    return lax.ppermute(v, "tensor", [(1, 2), (2, 1)])


def outward(v):
    return lax.ppermute(v, "tensor", [(1, 0), (2, 3)])


def swap(v, axis, bit):
    return lax.ppermute(v, axis, [(i, i ^ bit) for i in range(lax.axis_size(axis))])


def add_rounded(a, b):
    return (a.astype(F32) + b.astype(F32)).astype(BF16)


def after(first, value):
    return lax.optimization_barrier((first, value))[1]


class Order:
    def __init__(self):
        self.last = None

    def __call__(self, step, value, *rest):
        if self.last is not None:
            value = after(self.last, value)
        out = step(value, *rest)
        leaves = jax.tree.leaves(out)
        self.last = min(leaves, key=lambda a: a.size)
        return out


def halve(v, left, bit, run):
    me = lax.axis_index("dp")
    axis = left.index(bit)
    mine = (me >> bit) & 1
    sent = run(lambda a: lax.dynamic_index_in_dim(a, 1 - mine, axis, keepdims=False), v)
    got = swap(sent, "dp", 1 << bit)

    def add(got):
        return add_rounded(lax.dynamic_index_in_dim(v, mine, axis, keepdims=False), got)

    return got, add, [b for b in left if b != bit]


class ScatterSum:
    def __init__(self, value, split, run):
        self.run, self.split = run, split
        count = lax.axis_size("dp")
        bits = count.bit_length() - 1
        rows, columns = value.shape
        value = value.reshape((2,) * bits + (rows // count, columns))
        self.got, self.add, self.left = halve(value, list(range(bits - 1, -1, -1)), 0, run)

    def second(self):
        value = self.run(self.add, self.got)
        self.parts = []
        for part, order in zip(
            (value[..., : self.split], value[..., self.split :]), (self.left[::-1], self.left)
        ):
            got, add, rest = halve(part, self.left, order[0], self.run)
            self.parts.append((got, add, rest, order[1:]))

    def third(self):
        more = []
        for got, add, rest, order in self.parts:
            part = self.run(add, got)
            if order:
                got, add, rest = halve(part, rest, order[0], self.run)
                more.append((got, add, rest, order[1:]))
            else:
                more.append((part, None, rest, order))
        self.parts = more

    def finish(self):
        while self.parts[0][1] is not None:
            self.third()
        return [p[0].astype(F32) for p in self.parts]


def body(
    inputs, cotangent, row_expert, row_keep, window_resolution, attention_norm_gain,
    attention_norm_bias, qkv_weight, qv_bias, out_weight, out_bias, second_gain,
    expert_norm_bias, up_weight, up_bias, down_weight, down_bias,
):
    row_count, model = inputs.shape
    experts = up_weight.shape[0]
    width = qkv_weight.shape[2]
    windows = row_count // S
    tiles = S // TILE
    me = lax.axis_index("tensor")
    low = me < 2
    at_end = (me == 0) | (me == 3)
    low_int = low.astype(jnp.int32)
    place = lax.axis_index("dp")
    turn = ((place >> 1) & 1) + 2 * (place & 1)
    role = jnp.stack(
        [at_end.astype(jnp.int32), 1 - low_int, low_int, me, me ^ 2, me ^ 1, me ^ 3]
        + [turn, turn ^ 1, turn ^ 2, turn ^ 3]
    )
    run = Order()

    wt = jnp.transpose(qkv_weight, (0, 2, 1)).reshape(3 * width, model)
    pack = jnp.concatenate([wt, out_weight], 0)
    part = lax.dynamic_slice_in_dim(pack, turn * width, width, 0)
    part = swap(part, "tensor", 2)
    wo_far = swap(out_weight, "tensor", 1)
    bias_pair = qv_bias.reshape(2, width)
    bias_row = jnp.concatenate([bias_pair[0], jnp.zeros((width,), F32), bias_pair[1]])
    wb = jnp.broadcast_to(bias_row[None, :], (8, 3 * width))
    wb_c = swap(wb, "tensor", 2)
    every = range(windows)
    lanes = lambda v: v.reshape(windows, 1, S)
    kind = lax.broadcasted_iota(jnp.int32, (windows, 8, S), 1)
    upper = lax.broadcasted_iota(jnp.int32, (windows, 8, S), 2) >= S // 2
    alike = (window_resolution.reshape(windows, 1, 1) > 0) | (upper == (kind == 2))
    bias = jnp.where((lanes(row_keep) > 0) & alike, 0.0, MASKED).astype(F32)
    facts = jnp.where(kind == 0, lanes(row_expert).astype(F32), bias)
    xs, cots = [], []
    for w in every:
        at = slice(w * S, (w + 1) * S)
        xs.append(inputs[at])
        cots.append(cotangent[at])
    first = row_expert.reshape(2 * windows, S // 2)[:, 0]
    norm1 = (attention_norm_gain.reshape(1, model), attention_norm_bias.reshape(1, model))
    ob = out_bias.reshape(1, model)

    def do_own(w):
        return run(lambda x: attn_own(x, facts[w], *norm1, wt, wb), xs[w])

    def do_comp(w):
        given = (near, far, wt, out_weight) if w == 0 else (None, None, wt_c, None)
        return run(
            lambda n: attn_comp(w == 0, role, *given, (own[w][0], n, *own[w][2:]), own[w][4], wb_c),
            own[w][1],
        )

    own = [do_own(0)]
    part = after(run.last, part)
    other = swap(part, "dp", 2)
    own.append(do_own(1))
    near = run(lambda o: jnp.concatenate([part, o], 0), other)
    far = swap(near, "dp", 1)
    own.append(do_own(2))
    cols = [own[w][4] for w in every]
    comp = [do_comp(0)]
    wt_c, wt_both, wo_both, wo_c = comp[0][3:]
    wo = (wo_both, wo_far, swap(wo_c, "tensor", 1))
    mix_far = [swap(comp[0][2], "tensor", 1)]
    for w in (1, 2):
        comp.append(do_comp(w))
        mix_far.append(swap(comp[w][2], "tensor", 1))

    ex, gn2_in, s2, ga, bwd = ([None] * windows for _ in range(5))
    part_in, s_out, lo, sums, rows_grad = ([None] * windows for _ in range(5))

    def do_experts(w):
        def step(far_mix):
            return expert_fwd_bwd(
                w, role, first, window_resolution, comp[w][2], far_mix, wo, xs[w],
                cots[w], cols[w], ob, second_gain, expert_norm_bias, up_bias, up_weight, down_weight,
            )

        ex[w] = run(step, mix_far[w])
        gn2_in[w] = inward(ex[w][6])

    def do_sum2(w):
        s2[w] = run(add_rounded, gn2_in[w], ex[w][6])

    def do_mid(w):
        ga[w] = run(
            lambda r: mid_back(s2[w], r, ex[w][1], cots[w], cols[w], second_gain), across(s2[w])
        )

    def do_bwd(w):
        lse, qkv, mix = comp[w][:3]
        bwd[w] = run(
            lambda far: attn_bwd(role, ga[w], far, cols[w], wt_both, wo_both, mix, qkv, lse),
            outward(ga[w]),
        )

    def do_first(w):
        gn1, _, gaf = bwd[w]
        rows_grad[w], sums[w] = run(
            lambda r: first_back(gn1, r, gaf, xs[w], norm1[0]), swap(gn1, "tensor", 1)
        )

    def start_out(w):
        part_in[w] = inward(after(run.last, ex[w][5]))

    def do_out_sum(w):
        s_out[w] = run(add_rounded, part_in[w], ex[w][5])

    def do_out(w):
        lo[w] = run(
            lambda r: layer_out_rows(s_out[w], r, ex[w][1], cols[w], down_bias), across(s_out[w])
        )

    do_experts(0)
    do_experts(1)
    do_sum2(0)
    do_experts(2)
    start_out(0)
    small = run(lambda a, b, c: a + b + c, ex[2][0], ex[0][0], ex[1][0])
    shared = small[: 2 * experts]
    other = swap(shared, "tensor", 1)
    do_sum2(1)
    do_mid(0)
    shared = run(lambda o: shared + o, other)
    other = swap(shared, "tensor", 2)
    do_sum2(2)
    do_mid(1)
    do_bwd(0)
    start_out(1)
    shared = run(lambda o: shared + o, other)
    do_out_sum(0)
    do_mid(2)
    do_bwd(1)
    start_out(2)
    do_first(0)
    groups = [(*ex[w][2:5], cots[w], cols[w]) for w in every]
    expert_g = run(lambda f: expert_grads(f, window_resolution, groups, experts), first)
    eg = ScatterSum(expert_g, experts * up_weight.shape[2], run)
    do_out(0)
    do_out_sum(1)
    eg.second()
    do_bwd(2)
    eg.third()
    do_first(1)
    do_out(1)
    groups = [(own[w][1], bwd[w][1], own[w][3], bwd[w][2]) for w in every]
    attn_g, col_sums = run(lambda r: attn_grads(r, groups), role)
    up_g, down_g = eg.finish()
    ag = ScatterSum(attn_g, 3 * width, run)
    do_out_sum(2)
    ag.second()
    do_first(2)
    ag.third()
    do_out(2)
    qkv_g, out_g = ag.finish()
    outs = [jnp.where(at_end, outward(lo[w]), lo[w]) for w in every]

    totals = jnp.concatenate(
        [
            shared,
            small[2 * experts :],
            (sums[0] + sums[1] + sums[2])[:3],
            jnp.pad(col_sums[:1], ((0, 0), (0, model - 3 * width))),
        ],
        0,
    )
    for b in range(lax.axis_size("dp").bit_length() - 1):
        totals = totals + swap(totals, "dp", 1 << b)
    block = up_g.shape[0]
    hidden = up_weight.shape[2]
    grad_up = jnp.transpose(up_g.reshape(block, experts, hidden), (1, 0, 2))
    grad_down = jnp.transpose(down_g.reshape(block, experts, hidden), (1, 2, 0))
    grad_qkv = jnp.transpose(qkv_g.reshape(block, 3, width), (1, 0, 2))
    grad_out = out_g.T
    col = totals[4 * experts + 3]
    qv_grad = jnp.stack([col[:width], col[2 * width : 3 * width]]).reshape(qv_bias.shape)
    return (
        jnp.concatenate(outs, 0),
        jnp.concatenate(rows_grad, 0),
        totals[4 * experts],
        totals[4 * experts + 1],
        grad_qkv,
        qv_grad,
        grad_out,
        totals[4 * experts + 2],
        totals[:experts],
        totals[experts : 2 * experts],
        grad_up,
        totals[2 * experts : 3 * experts],
        grad_down,
        totals[3 * experts : 4 * experts],
    )


def solution(mesh):
    in_specs = (
        P("dp", None), P("dp", None), P("dp"), P("dp"), P("dp"), P(), P(),
        P(None, None, "tensor"), P(None, "tensor", None), P("tensor", None), P(), P(), P(),
        P(None, None, "tensor"), P(None, "tensor"), P(None, "tensor", None), P(),
    )
    out_specs = (
        P("dp", None), P("dp", None), P(), P(), P(None, "dp", "tensor"), P(None, "tensor", None),
        P("tensor", "dp"), P(), P(), P(), P(None, "dp", "tensor"), P(None, "tensor"),
        P(None, "tensor", "dp"), P(),
    )
    return jax.shard_map(body, mesh=mesh, in_specs=in_specs, out_specs=out_specs, check_vma=False)
```

```python
import functools
import math

import jax
import jax.numpy as jnp
from jax import lax
from jax.experimental import pallas as pl
from jax.experimental.pallas import tpu as pltpu
from jax.sharding import PartitionSpec as P

HEAD_DIM = 64
S = 768
TILE = 192
BACK = 656
ROLES = [[int(t in (0, 3)), int(t > 1), int(t < 2), t, t ^ 2, t ^ 1, t ^ 3] for t in range(4)]
EXPERT_MIB = 32
GRADS_MIB = 20
EPS = 1e-05
MASKED = -1000000000.0
SCALE = 1.0 / math.sqrt(HEAD_DIM)
F32 = jnp.float32
BF16 = jnp.bfloat16

NN = (((1,), (0,)), ((), ()))
NT = (((1,), (1,)), ((), ()))
TN = (((0,), (0,)), ((), ()))


def mm(a, b, dims=NN):
    return lax.dot_general(a, b, dims, preferred_element_type=F32)


def row_mean(v):
    lanes = 128
    total = v[:, 0:lanes]
    for i in range(1, v.shape[1] // lanes):
        total = total + v[:, i * lanes : (i + 1) * lanes]
    return jnp.sum(total, -1, keepdims=True) * (1.0 / v.shape[1])


def layer_norm(values):
    centred = values - row_mean(values)
    rstd = lax.rsqrt(row_mean(centred * centred) + EPS)
    return centred * rstd, rstd


def norm_back(scaled, xhat, rstd):
    return rstd * (scaled - row_mean(scaled) - xhat * row_mean(scaled * xhat))


def pick_rows(table_ref, expert):
    out = jnp.where(expert == 0, table_ref[0:1, :], table_ref[1:2, :])
    return jnp.where(expert == 2, table_ref[2:3, :], out)


def cost(flops=1e6):
    return pl.CostEstimate(flops=int(flops), bytes_accessed=1, transcendentals=0)


def window(w, n, rows=S):
    return pl.BlockSpec((rows, n), lambda i: (w, 0))


def full(a):
    return pl.BlockSpec(a.shape, lambda i: (0,) * a.ndim)


def params(mib):
    return pltpu.CompilerParams(vmem_limit_bytes=mib * 1024 * 1024)


def heads_forward(qkv_ref, cols_ref, mix_ref, lse_ref, base):
    width = qkv_ref.shape[0] // 3
    first = base // HEAD_DIM
    half = S // 2
    for h in range(width // HEAD_DIM):
        kt = qkv_ref[pl.ds(width + h * HEAD_DIM, HEAD_DIM), :]
        vt = qkv_ref[pl.ds(2 * width + h * HEAD_DIM, HEAD_DIM), :]
        k = kt.T
        for c in range(2):
            at = pl.ds(c * half, half)
            qt = qkv_ref[pl.ds(h * HEAD_DIM, HEAD_DIM), at]
            s = mm(k, qt) + cols_ref[:, c + 1 : c + 2]
            top = jnp.max(s, 0, keepdims=True)
            p = jnp.exp(s - top)
            total = jnp.sum(p, 0, keepdims=True)
            o = mm(vt, p.astype(BF16)) * (1.0 / total)
            mix_ref[pl.ds(base + h * HEAD_DIM, HEAD_DIM), at] = o.astype(BF16)
            lse_ref[pl.ds(first + h, 1), at] = top + jnp.log(total)


def project(wt_ref, wb_ref, normed, qkv_ref):
    width = wt_ref.shape[0] // 3
    bias = jnp.concatenate([wb_ref[...], jnp.zeros((6, width), F32)], 0).T
    for j in range(3):
        rows = pl.ds(j * width, width)
        part = mm(wt_ref[rows, :], normed, NT)
        if j != 1:
            part = part + bias[:, j // 2 : j // 2 + 1]
        part = part.astype(BF16)
        if j == 0:
            part = part * jnp.asarray(SCALE, BF16)
        qkv_ref[rows, :] = part


HBM = pl.BlockSpec(memory_space=pltpu.HBM)
SMEM = pl.BlockSpec(memory_space=pltpu.SMEM)
VMEM = pl.BlockSpec(memory_space=pltpu.VMEM)


def start(source, target, sem):
    copy = pltpu.make_async_copy(source, target, sem)
    copy.start()
    return copy


def attn_own_kernel(
    w, res_ref, x_ref, expert_ref, keep_ref, consts_ref, wt_ref, wb_ref, lse_ref, n1_ref, qkv_ref, mix_ref, cols_ref
):
    kind = lax.broadcasted_iota(jnp.int32, (8, S), 0)
    upper = lax.broadcasted_iota(jnp.int32, (8, S), 1) >= S // 2
    alike = jnp.logical_or(res_ref[w] > 0, upper == (kind == 2))
    seen = jnp.logical_and(keep_ref[w : w + 1, :] > 0, alike)
    facts = jnp.where(kind == 0, expert_ref[w : w + 1, :].astype(F32), jnp.where(seen, 0.0, MASKED))
    cols_ref[...] = facts.T
    xhat, _ = layer_norm(x_ref[...].astype(F32))
    n1_ref[...] = (xhat * consts_ref[0:1, :] + consts_ref[1:2, :]).astype(BF16)
    project(wt_ref, wb_ref, n1_ref[...], qkv_ref)
    heads_forward(qkv_ref, cols_ref, mix_ref, lse_ref, 0)


def attn_own(w, res, x, expert, keep, consts, wt, wb):
    rows, model = x.shape
    width = wt.shape[0] // 3
    return pl.pallas_call(
        functools.partial(attn_own_kernel, w),
        out_shape=(
            jax.ShapeDtypeStruct((width // HEAD_DIM, rows), F32),
            jax.ShapeDtypeStruct((rows, model), BF16),
            jax.ShapeDtypeStruct((3 * width, rows), BF16),
            jax.ShapeDtypeStruct((width, rows), BF16),
            jax.ShapeDtypeStruct((rows, 8), F32),
        ),
        in_specs=[SMEM] + [VMEM] * 6,
        out_specs=(VMEM,) * 5,
        compiler_params=params(9),
        cost_estimate=cost(),
        name="attn_own",
    )(res, x, expert, keep, consts, wt, wb)


def attn_comp_kernel(
    emit, role_ref, near_ref, far_ref, wt_ref, wo_ref, n1_ref, own_qkv_ref, own_ref, own_lse_ref, cols_ref, wb_ref,
    lse_ref, qkv_ref, mix_ref, *refs
):
    width = own_ref.shape[0]
    wide = 3 * width
    heads = width // HEAD_DIM
    if emit:
        wt_c_ref, wt_both_ref, wo_both_ref, wo_c_ref, pack_v = refs
        for j in range(4):
            at = pl.ds(pl.multiple_of(role_ref[7 + j] * width, width), width)
            pack_v[at, :] = (near_ref, far_ref)[j // 2][(j % 2) * width : (j % 2 + 1) * width, :]
        wt_c_ref[...] = pack_v[0:wide, :]
        wo_both_ref[0:width, :] = wo_ref[...]
        wo_both_ref[width:, :] = pack_v[wide:, :]
        wo_c_ref[...] = pack_v[wide:, :]
        wt_both_ref[pl.ds(pl.multiple_of(role_ref[1] * wide, wide), wide), :] = wt_ref[...]
        wt_both_ref[pl.ds(pl.multiple_of(role_ref[2] * wide, wide), wide), :] = pack_v[0:wide, :]
        weights = wt_c_ref
    else:
        weights = wt_ref
    qkv_ref[0:wide, :] = own_qkv_ref[...]
    mix_ref[0:width, :] = own_ref[...]
    lse_ref[0:heads, :] = own_lse_ref[...]
    comp = qkv_ref.at[pl.ds(wide, wide), :]
    project(weights, wb_ref, n1_ref[...], comp)
    heads_forward(comp, cols_ref, mix_ref, lse_ref, width)


def attn_comp(emit, role, near, far, wt, wo, own, cols, wb):
    own_lse, n1, own_qkv, own_mix = own[:4]
    rows, model = n1.shape
    width = own_mix.shape[0]
    outs = [
        jax.ShapeDtypeStruct((2 * (width // HEAD_DIM), rows), F32),
        jax.ShapeDtypeStruct((6 * width, rows), BF16),
        jax.ShapeDtypeStruct((2 * width, rows), BF16),
    ]
    if emit:
        outs += [
            jax.ShapeDtypeStruct((3 * width, model), BF16),
            jax.ShapeDtypeStruct((6 * width, model), BF16),
            jax.ShapeDtypeStruct((2 * width, model), BF16),
            jax.ShapeDtypeStruct((width, model), BF16),
        ]
    given = (near, far, wt, wo) if emit else (wt,)
    kernel = functools.partial(attn_comp_kernel, True) if emit else attn_comp_later
    return pl.pallas_call(
        kernel,
        out_shape=tuple(outs),
        in_specs=[SMEM] + [VMEM] * (len(given) + 6),
        out_specs=(VMEM,) * len(outs),
        scratch_shapes=[pltpu.VMEM((4 * width, model), BF16)] if emit else [],
        compiler_params=params(9),
        cost_estimate=cost(),
        name="attn_comp",
    )(role, *given, n1, own_qkv, own_mix, own_lse, cols, wb)


def attn_comp_later(role_ref, wt_ref, *refs):
    attn_comp_kernel(False, role_ref, None, None, wt_ref, None, *refs)


def attn_both_kernel(
    w, res_ref, x_ref, expert_ref, keep_ref, consts_ref, wt_ref, wb_ref, wt_c_ref, wb_c_ref,
    lse_ref, n1_ref, qkv_ref, mix_ref, cols_ref,
):
    wide = wt_ref.shape[0]
    own = qkv_ref.at[pl.ds(0, wide), :]
    attn_own_kernel(
        w, res_ref, x_ref, expert_ref, keep_ref, consts_ref, wt_ref, wb_ref, lse_ref, n1_ref, own, mix_ref, cols_ref
    )
    comp = qkv_ref.at[pl.ds(wide, wide), :]
    project(wt_c_ref, wb_c_ref, n1_ref[...], comp)
    heads_forward(comp, cols_ref, mix_ref, lse_ref, wide // 3)


def attn_both(w, res, x, expert, keep, consts, wt, wb, wt_c, wb_c):
    rows, model = x.shape
    width = wt.shape[0] // 3
    return pl.pallas_call(
        functools.partial(attn_both_kernel, w),
        out_shape=(
            jax.ShapeDtypeStruct((2 * (width // HEAD_DIM), rows), F32),
            jax.ShapeDtypeStruct((rows, model), BF16),
            jax.ShapeDtypeStruct((6 * width, rows), BF16),
            jax.ShapeDtypeStruct((2 * width, rows), BF16),
            jax.ShapeDtypeStruct((rows, 8), F32),
        ),
        in_specs=[SMEM] + [VMEM] * 8,
        out_specs=(VMEM,) * 5,
        compiler_params=params(10),
        cost_estimate=cost(),
        name="attn_both",
    )(res, x, expert, keep, consts, wt, wb, wt_c, wb_c)


def present(first_ref, res_ref, w, tile, e):
    single = res_ref[w] > 0
    second = jnp.logical_and(jnp.logical_not(single), tile >= (S // TILE) // 2)
    image = first_ref[2 * w + second.astype(jnp.int32)]
    mixed = tile == S // TILE - 1
    mixed = jnp.logical_or(mixed, jnp.logical_and(jnp.logical_not(single), tile == (S // TILE) // 2 - 1))
    return jnp.logical_or(e == image, jnp.logical_and(mixed, e == 1))


def expert_kernel(
    w, role_ref, first_ref, res_ref, mix_ref, far_ref, wo_ref, wo_far_ref, wo_far_comp_ref, x_ref, cot_v,
    cols_ref, ob_ref, g2_ref, b2_ref, ub_ref, up_v, down_v,
    small_ref, mid_ref, n2_v, act_v, gpre_v, out_v, gn2_ref,
    mix_v, wo_v, xhat_v, gn2_v,
):
    experts = up_v.shape[0]
    width = mix_ref.shape[0] // 2
    tiles = S // TILE
    for j in range(4):
        at = pl.ds(pl.multiple_of(role_ref[3 + j] * width, width), width)
        piece = slice((j % 2) * width, (j % 2 + 1) * width)
        mix_v[at, :] = (mix_ref, far_ref)[j // 2][piece, :]
        wo_v[at, :] = wo_ref[piece, :] if j < 2 else (wo_far_ref, wo_far_comp_ref)[j - 2][...]
    expert = cols_ref[:, 0:1]
    small_ref[...] = jnp.zeros_like(small_ref)
    proj = mm(mix_v[...], wo_v[...], TN)
    middle = x_ref[...].astype(F32) + (proj + ob_ref[2:3, :])
    mid_ref[...] = middle.astype(BF16)
    xhat, _ = layer_norm(middle)
    xhat_v[...] = xhat
    n2_v[...] = (xhat * pick_rows(g2_ref, expert) + pick_rows(b2_ref, expert)).astype(BF16)

    def tile_step(tile, carry):
        at = pl.ds(pl.multiple_of(tile * TILE, TILE), TILE)
        for ref in (act_v, gpre_v, out_v, gn2_v):
            ref[at, :] = jnp.zeros((TILE, ref.shape[1]), BF16)

        def step(e, carry):
            @pl.when(present(first_ref, res_ref, w, tile, e))
            def _():
                mask = (cols_ref[at, 0:1] == e.astype(F32)).astype(F32)
                cot = cot_v[at, :]
                pre = mm(n2_v[at, :], up_v[e]) + ub_ref[pl.ds(e, 1), :]
                cdf = 0.5 + 0.5 * lax.erf(pre * (1.0 / math.sqrt(2.0)))
                act = (pre * cdf * mask).astype(BF16)
                slope = cdf + pre * (jnp.exp(-0.5 * pre * pre) * (1.0 / math.sqrt(2.0 * math.pi)))
                gpre = (mm(cot, down_v[e], NT) * slope * mask).astype(BF16)
                gn2 = mm(gpre, up_v[e], NT)
                out = mm(act, down_v[e])
                act_v[at, :] = act_v[at, :] + act
                gpre_v[at, :] = gpre_v[at, :] + gpre
                out_v[at, :] = out_v[at, :] + out.astype(BF16)
                gn2_v[at, :] = gn2_v[at, :] + gn2.astype(BF16)
                for j, values in enumerate(
                    (gn2 * xhat_v[at, :], gn2, gpre.astype(F32), cot.astype(F32) * mask)
                ):
                    row = pl.ds(j * experts + e, 1)
                    small_ref[row, :] = small_ref[row, :] + jnp.sum(values, 0, keepdims=True)

            return carry

        lax.fori_loop(0, experts, step, 0)
        return carry

    lax.fori_loop(0, tiles, tile_step, 0)
    gn2_ref[...] = gn2_v[0:BACK, :]


def expert_fwd_bwd(w, role, first, res, mix, far, wo, x, cot, cols, ob, g2, b2, ub, up, down):
    rows, model = x.shape
    experts, _, hidden = up.shape
    return pl.pallas_call(
        functools.partial(expert_kernel, w),
        out_shape=(
            jax.ShapeDtypeStruct((4 * experts, model), F32),
            jax.ShapeDtypeStruct((rows, model), BF16),
            jax.ShapeDtypeStruct((rows, model), BF16),
            jax.ShapeDtypeStruct((rows, hidden), BF16),
            jax.ShapeDtypeStruct((rows, hidden), BF16),
            jax.ShapeDtypeStruct((rows, model), BF16),
            jax.ShapeDtypeStruct((BACK, model), BF16),
        ),
        in_specs=[SMEM] * 3 + [VMEM] * 14,
        out_specs=(VMEM,) * 7,
        scratch_shapes=[
            pltpu.VMEM((rows, model), BF16),
            pltpu.VMEM((rows, model), BF16),
            pltpu.VMEM((rows, model), F32),
            pltpu.VMEM((rows, model), BF16),
        ],
        compiler_params=params(22),
        cost_estimate=cost(1e11),
        name="expert_fwd_bwd",
    )(role, first, res, mix, far, *wo, x, cot, cols, ob, g2, b2, ub, up, down)


def expert_grads_kernel(windows, first_ref, res_ref, *refs):
    groups = [refs[5 * w : 5 * w + 5] for w in range(windows)]
    out_ref, acc = refs[-2:]
    e, kind = pl.program_id(0), pl.program_id(1)
    tiles = S // TILE
    acc[...] = jnp.zeros_like(acc)

    def add(cols_ref, row, count, left, right):
        at = pl.ds(pl.multiple_of(row, TILE), count)
        mask = (cols_ref[at, 0:1] == e.astype(F32)).astype(BF16)
        acc[...] += mm(left[at, :], right[at, :] * mask, TN)

    def half_step(w, half, carry):
        n2_ref, act_ref, gpre_ref, cot_ref, cols_ref = groups[w]
        tile = 2 * half
        row = tile * TILE
        here = present(first_ref, res_ref, w, tile, e)
        next_ = present(first_ref, res_ref, w, tile + 1, e)
        for k, (left, right) in enumerate(((n2_ref, gpre_ref), (cot_ref, act_ref))):

            @pl.when(jnp.logical_and(kind == k, jnp.logical_and(here, next_)))
            def _():
                add(cols_ref, row, 2 * TILE, left, right)

            @pl.when(jnp.logical_and(kind == k, here != next_))
            def _():
                add(cols_ref, row + jnp.where(here, 0, TILE), TILE, left, right)

        return carry

    for w in range(windows):
        lax.fori_loop(0, tiles // 2, functools.partial(half_step, w), 0)
    out_ref[...] = acc[...].astype(BF16)


def expert_grads(first, res, groups, experts):
    model = groups[0][0].shape[1]
    hidden = groups[0][1].shape[1]
    flat = [a for g in groups for a in g]
    return pl.pallas_call(
        functools.partial(expert_grads_kernel, len(groups)),
        grid=(experts, 2),
        out_shape=jax.ShapeDtypeStruct((model, 2 * experts * hidden), BF16),
        in_specs=[SMEM] * 2 + [VMEM] * len(flat),
        out_specs=pl.BlockSpec((model, hidden), lambda e, k: (0, k * experts + e)),
        scratch_shapes=[pltpu.VMEM((model, hidden), F32)],
        compiler_params=params(9),
        cost_estimate=cost(1e11),
        name="expert_grads",
    )(first, res, *flat)


def mid_back_kernel(s_ref, r_ref, mid_ref, cot_ref, cols_ref, g2_ref, ga_ref):
    top = slice(0, BACK)
    total = s_ref[...].astype(F32) + r_ref[...].astype(F32)
    xhat, rstd = layer_norm(mid_ref[top, :].astype(F32))
    gain = pick_rows(g2_ref, cols_ref[top, 0:1])
    grad = cot_ref[top, :].astype(F32) + norm_back(total * gain, xhat, rstd)
    ga_ref[...] = grad.astype(BF16)


def mid_back(s, r, mid, cot, cols, g2):
    return pl.pallas_call(
        mid_back_kernel,
        out_shape=jax.ShapeDtypeStruct(s.shape, BF16),
        in_specs=[VMEM] * 6,
        out_specs=VMEM,
        compiler_params=params(10),
        cost_estimate=cost(1e11),
        name="mid_back",
    )(s, r, mid, cot, cols, g2)


def attn_bwd_kernel(
    role_ref, ga_ref, far_ref, cols_ref, wt_ref, wo_ref, mix_ref, qkv_ref, lse_ref,
    gn1_ref, dqkv_ref, gaf_ref, gmt_v,
):
    width = wo_ref.shape[0] // 2
    wide = 3 * width
    heads = width // HEAD_DIM
    take = role_ref[0] > 0
    top = pl.ds(0, BACK)

    @pl.when(take)
    def _():
        gaf_ref[top, :] = far_ref[...]

    @pl.when(jnp.logical_not(take))
    def _():
        gaf_ref[top, :] = ga_ref[...]

    gaf_ref[BACK:, :] = jnp.zeros((S - BACK, gaf_ref.shape[1]), BF16)
    gmt_v[...] = mm(wo_ref[...], gaf_ref[...], NT).astype(BF16)
    half = S // 2

    def group(g, carry):
        into = role_ref[1 + g] * wide
        for h in range(heads):
            at = lambda base, step: pl.ds(pl.multiple_of(base + h * HEAD_DIM, HEAD_DIM), HEAD_DIM)
            both = at(g * width, 0)
            q_rows, k_rows, v_rows = (at(g * wide + j * width, 0) for j in range(3))
            q_into, k_into, v_into = (at(into + j * width, 0) for j in range(3))
            kt, vt = qkv_ref[k_rows, :], qkv_ref[v_rows, :]
            k, v = kt.T, vt.T
            row = pl.ds(g * heads + h, 1)
            dk = dv = None
            for c in range(2):
                part = pl.ds(c * half, half)
                qt = qkv_ref[q_rows, part]
                dot = gmt_v[both, part]
                delta = jnp.sum(dot.astype(F32) * mix_ref[both, part].astype(F32), 0, keepdims=True)
                s = mm(k, qt) + cols_ref[:, c + 1 : c + 2]
                p = jnp.exp(s - lse_ref[row, part])
                ds = (p * (mm(v, dot) - delta)).astype(BF16)
                dv_c = mm(p.astype(BF16), dot, NT)
                dk_c = mm(ds, qt, NT)
                dv = dv_c if dv is None else dv + dv_c
                dk = dk_c if dk is None else dk + dk_c
                dqkv_ref[q_into, part] = (mm(kt, ds) * SCALE).astype(BF16)
            dqkv_ref[k_into, :] = dk.astype(BF16).T
            dqkv_ref[v_into, :] = dv.astype(BF16).T
        return carry

    lax.fori_loop(0, 2, group, 0)
    gn1_ref[...] = mm(dqkv_ref[:, 0:BACK], wt_ref[...], TN).astype(BF16)


def attn_bwd(role, ga, far, cols, wt, wo, mix, qkv, lse):
    model = wo.shape[1]
    return pl.pallas_call(
        attn_bwd_kernel,
        out_shape=(
            jax.ShapeDtypeStruct((BACK, model), BF16),
            jax.ShapeDtypeStruct(qkv.shape, BF16),
            jax.ShapeDtypeStruct((S, model), BF16),
        ),
        in_specs=[SMEM] + [VMEM] * 8,
        out_specs=(VMEM,) * 3,
        scratch_shapes=[pltpu.VMEM(mix.shape, BF16)],
        compiler_params=params(11),
        cost_estimate=cost(1e11),
        name="attn_bwd",
    )(role, ga, far, cols, wt, wo, mix, qkv, lse)


def attn_grads_kernel(role_ref, *refs):
    windows = (len(refs) - 8) // 4
    groups = [refs[4 * w : 4 * w + 4] for w in range(windows)]
    out_ref, sum_ref, n1_v, gaf_v, dqkv_v, mix_v, acc, sems = refs[-8:]
    wide = dqkv_v.shape[0]
    own = pl.ds(pl.multiple_of(role_ref[1] * wide, wide), wide)
    loads = []
    for w, (n1_ref, dqkv_ref, mix_ref, gaf_ref) in enumerate(groups):
        at = pl.ds(w * S, S)
        pairs = (
            (dqkv_ref.at[own, :], dqkv_v.at[:, at]),
            (n1_ref, n1_v.at[at, :]),
            (mix_ref.at[pl.ds(0, mix_v.shape[0]), :], mix_v.at[:, at]),
            (gaf_ref, gaf_v.at[at, :]),
        )
        loads += [start(a, b, sems.at[4 * w + j]) for j, (a, b) in enumerate(pairs)]
    for load in loads:
        load.wait()
    acc[0:wide, :] = mm(dqkv_v[...], n1_v[...])
    acc[wide:, :] = mm(mix_v[...], gaf_v[...])
    sum_ref[...] = mm(jnp.ones((8, dqkv_v.shape[1]), BF16), dqkv_v[...], NT)
    out_ref[...] = acc[...].astype(BF16).T


def attn_grads(role, groups):
    n1, dqkv = groups[0][:2]
    model = n1.shape[1]
    wide = dqkv.shape[0] // 2
    rows = len(groups) * S
    flat = [a for g in groups for a in g]
    outs = (
        jax.ShapeDtypeStruct((model, wide + wide // 3), BF16),
        jax.ShapeDtypeStruct((8, wide), F32),
    )
    return pl.pallas_call(
        attn_grads_kernel,
        grid=(1,),
        out_shape=outs,
        in_specs=[SMEM] + [HBM] * len(flat),
        out_specs=tuple(full(o) for o in outs),
        scratch_shapes=[
            pltpu.VMEM((rows, model), BF16),
            pltpu.VMEM((rows, model), BF16),
            pltpu.VMEM((wide, rows), BF16),
            pltpu.VMEM((wide // 3, rows), BF16),
            pltpu.VMEM((wide + wide // 3, model), F32),
            pltpu.SemaphoreType.DMA((4 * len(groups),)),
        ],
        compiler_params=params(50),
        cost_estimate=cost(1e11),
        name="attn_grads",
    )(role, *flat)


def first_back_kernel(w, s_ref, r_ref, ga_ref, x_ref, g_ref, *refs):
    out_ref, sum_ref, out_v, sem = refs[-4:]
    top = slice(0, BACK)
    total = s_ref[...].astype(F32) + r_ref[...].astype(F32)
    xhat, rstd = layer_norm(x_ref[top, :].astype(F32))
    ga = ga_ref[top, :].astype(F32)
    back = norm_back(total * g_ref[0:1, :], xhat, rstd)
    out_v[top, :] = (ga + back).astype(BF16)
    out_v[BACK:, :] = jnp.zeros((S - BACK, out_v.shape[1]), BF16)
    copy = start(out_v, out_ref.at[pl.ds(w * S, S), :], sem)
    sum_ref[...] = jnp.zeros_like(sum_ref)
    for j, values in enumerate((total * xhat, total, ga)):
        sum_ref[j : j + 1, :] = jnp.sum(values, 0, keepdims=True)
    copy.wait()


def first_back(w, s, r, ga, x, g, rows, into):
    model = s.shape[1]
    more = () if into is None else (into,)
    return pl.pallas_call(
        functools.partial(first_back_kernel, w),
        out_shape=(
            jax.ShapeDtypeStruct((rows, model), BF16),
            jax.ShapeDtypeStruct((8, model), F32),
        ),
        in_specs=[VMEM] * 5 + [HBM] * len(more),
        out_specs=(HBM, VMEM),
        scratch_shapes=[pltpu.VMEM((S, model), BF16), pltpu.SemaphoreType.DMA],
        input_output_aliases={5: 0} if more else {},
        compiler_params=params(12),
        cost_estimate=cost(1e11),
        name="first_back",
    )(s, r, ga, x, g, *more)


def layer_out_kernel(s_ref, r_ref, mid_ref, cols_ref, db_ref, out_ref):
    total = s_ref[...].astype(F32) + r_ref[...].astype(F32)
    shift = pick_rows(db_ref, cols_ref[:, 0:1])
    out_ref[...] = (mid_ref[...].astype(F32) + (total + shift)).astype(BF16)


def layer_out_rows(s, r, mid, cols, db):
    return pl.pallas_call(
        layer_out_kernel,
        out_shape=jax.ShapeDtypeStruct(mid.shape, BF16),
        in_specs=[VMEM] * 5,
        out_specs=VMEM,
        compiler_params=params(10),
        cost_estimate=cost(1e11),
        name="layer_out_rows",
    )(s, r, mid, cols, db)


def place_kernel(w, role_ref, own_ref, far_ref, *refs):
    out_ref, out_v, sem = refs[-3:]

    @pl.when(role_ref[0] > 0)
    def _():
        out_v[...] = far_ref[...]

    @pl.when(role_ref[0] == 0)
    def _():
        out_v[...] = own_ref[...]

    start(out_v, out_ref.at[pl.ds(w * S, S), :], sem).wait()


def place_rows(w, role, own, far, rows, into):
    model = own.shape[1]
    more = () if into is None else (into,)
    return pl.pallas_call(
        functools.partial(place_kernel, w),
        out_shape=jax.ShapeDtypeStruct((rows, model), BF16),
        in_specs=[SMEM] + [VMEM] * 2 + [HBM] * len(more),
        out_specs=HBM,
        scratch_shapes=[pltpu.VMEM((S, model), BF16), pltpu.SemaphoreType.DMA],
        input_output_aliases={3: 0} if more else {},
        compiler_params=params(5),
        cost_estimate=cost(1e11),
        name="place_rows",
    )(role, own, far, *more)


def inward(v):
    return lax.ppermute(v, "tensor", [(0, 1), (3, 2)])


def across(v):
    return lax.ppermute(v, "tensor", [(1, 2), (2, 1)])


def outward(v):
    return lax.ppermute(v, "tensor", [(1, 0), (2, 3)])


def swap(v, axis, bit):
    return lax.ppermute(v, axis, [(i, i ^ bit) for i in range(lax.axis_size(axis))])


def add_rounded(a, b):
    return (a.astype(F32) + b.astype(F32)).astype(BF16)


def after(first, value):
    return lax.optimization_barrier((first, value))[1]


class Order:
    def __init__(self):
        self.last = None

    def __call__(self, step, value, *rest):
        if self.last is not None:
            value = after(self.last, value)
        out = step(value, *rest)
        leaves = jax.tree.leaves(out)
        self.last = min(leaves, key=lambda a: a.size)
        return out


def halve(value, left, bit, run):
    axis, mine = left.index(bit), (lax.axis_index("dp") >> bit) & 1
    sent = run(lambda v: lax.dynamic_index_in_dim(v, 1 - mine, axis, keepdims=False), value)
    got = swap(sent, "dp", 1 << bit)

    def add(got, value):
        return add_rounded(lax.dynamic_index_in_dim(value, mine, axis, keepdims=False), got)

    return value, got, add, [b for b in left if b != bit]


class ScatterSum:
    def __init__(self, value, widths, run):
        self.run, self.widths = run, widths
        count = lax.axis_size("dp")
        bits = count.bit_length() - 1
        rows, columns = value.shape
        value = value.reshape((2,) * bits + (rows // count, columns))
        self.parts = [(halve(value, list(range(bits - 1, -1, -1)), 0, run), 1)]

    def add(self):
        values = [(self.run(h[2], h[1], h[0]), h[3], way) for h, way in self.parts]
        if self.widths:
            value, left, _ = values[0]
            ends = [sum(self.widths[: k + 1]) for k in range(len(self.widths))]
            values = [
                (value[..., e - n : e], left, (-1) ** k)
                for k, (e, n) in enumerate(zip(ends, self.widths))
            ]
            self.widths = None
        if not values[0][1]:
            return [v.astype(F32) for v, _, _ in values]
        self.parts = [
            (halve(v, left, left[::-way][0], self.run), way) for v, left, way in values
        ]
        return None

    def finish(self):
        done = None
        while done is None:
            done = self.add()
        return done


def body(
    inputs, cotangent, row_expert, row_keep, window_resolution, attention_norm_gain,
    attention_norm_bias, qkv_weight, qv_bias, out_weight, out_bias, second_gain,
    expert_norm_bias, up_weight, up_bias, down_weight, down_bias,
):
    row_count, model = inputs.shape
    experts = up_weight.shape[0]
    width = qkv_weight.shape[2]
    windows = row_count // S
    tiles = S // TILE
    me = lax.axis_index("tensor")
    low = me < 2
    at_end = (me == 0) | (me == 3)
    place = lax.axis_index("dp")
    turn = ((place >> 1) & 1) + 2 * (place & 1)
    role = jnp.concatenate(
        [
            jnp.asarray(ROLES, jnp.int32)[me],
            turn ^ jnp.arange(4, dtype=jnp.int32),
        ]
    )
    run = Order()

    wt = jnp.transpose(qkv_weight, (0, 2, 1)).reshape(3 * width, model)
    pack = jnp.concatenate([wt, out_weight], 0)
    part = lax.dynamic_slice_in_dim(pack, turn * width, width, 0)
    part = swap(part, "tensor", 2)
    wo_far = swap(out_weight, "tensor", 1)
    wb = qv_bias.reshape(2, width)
    wb_c = swap(wb, "tensor", 2)
    every = range(windows)
    expert_rows, keep_rows = row_expert.reshape(windows, S), row_keep.reshape(windows, S)
    consts = jnp.stack([attention_norm_gain, attention_norm_bias, out_bias])
    at = [slice(w * S, (w + 1) * S) for w in every]
    xs, cots = [inputs[at[0]], None, None], [None] * windows

    given = (expert_rows, keep_rows, consts, wt, wb)
    own_lse, n1, own_qkv, own_mix, facts = run(
        lambda x: attn_own(0, window_resolution, x, *given), xs[0]
    )
    part = after(run.last, part)
    other = swap(part, "dp", 2)
    for w in every:
        cots[w] = run(lambda c: c[at[w]], cotangent)
        if w > 0:
            xs[w] = run(lambda c: c[at[w]], inputs)
    first = run(lambda e: e[:: S // 2], row_expert)
    near = run(lambda o: jnp.concatenate([part, o], 0), other)
    far = swap(near, "dp", 1)
    lse, qkv, mix, wt_c, wt_both, wo_both, wo_c = run(
        lambda f: attn_comp(
            True, role, near, f, wt, out_weight, (own_lse, n1, own_qkv, own_mix), facts, wb_c
        ),
        far,
    )
    wo = (wo_both, wo_far, swap(wo_c, "tensor", 1))
    fwd = [(lse, n1, qkv, mix, facts)]
    mix_far = [swap(mix, "tensor", 1)]
    for w in (1, 2):
        fwd.append(run(lambda x: attn_both(w, window_resolution, x, *given, wt_c, wb_c), xs[w]))
        mix_far.append(swap(fwd[w][3], "tensor", 1))
    cols = [fwd[w][4] for w in every]

    ex, gn2_in, s2, ga, bwd = ([None] * windows for _ in range(5))
    part_in, s_out, lo, sums = ([None] * windows for _ in range(4))

    def do_experts(w):
        def step(far_mix):
            return expert_fwd_bwd(
                w, role, first, window_resolution, fwd[w][3], far_mix, wo, xs[w],
                cots[w], cols[w], consts, second_gain, expert_norm_bias, up_bias, up_weight, down_weight,
            )

        ex[w] = run(step, mix_far[w])
        gn2_in[w] = inward(ex[w][6])

    def do_sum2(w):
        s2[w] = run(add_rounded, gn2_in[w], ex[w][6])

    def do_mid(w):
        ga[w] = run(
            lambda r: mid_back(s2[w], r, ex[w][1], cots[w], cols[w], second_gain), across(s2[w])
        )

    def do_bwd(w):
        lse, _, qkv, mix, _ = fwd[w]
        bwd[w] = run(
            lambda far: attn_bwd(role, ga[w], far, cols[w], wt_both, wo_both, mix, qkv, lse),
            outward(ga[w]),
        )

    def do_first(w, into):
        gn1, _, gaf = bwd[w]
        into, sums[w] = run(
            lambda r: first_back(w, gn1, r, gaf, xs[w], consts, row_count, into),
            swap(gn1, "tensor", 1),
        )
        return into

    def do_place(w, into):
        return run(lambda f: place_rows(w, role, lo[w], f, row_count, into), outward(lo[w]))

    def start_out(w):
        part_in[w] = inward(after(run.last, ex[w][5]))

    def do_out_sum(w):
        s_out[w] = run(add_rounded, part_in[w], ex[w][5])

    def do_out(w):
        lo[w] = run(
            lambda r: layer_out_rows(s_out[w], r, ex[w][1], cols[w], down_bias), across(s_out[w])
        )

    do_experts(0)
    do_experts(1)
    do_sum2(0)
    do_experts(2)
    start_out(0)
    small = run(lambda a, b, c: a + b + c, ex[2][0], ex[0][0], ex[1][0])
    shared = small[: 2 * experts]
    other = swap(shared, "tensor", 1)
    do_sum2(1)
    do_mid(0)
    do_sum2(2)
    do_mid(1)
    do_bwd(0)
    shared = run(lambda o: shared + o, other)
    other = swap(shared, "tensor", 2)
    start_out(1)
    do_out_sum(0)
    do_mid(2)
    do_bwd(1)
    shared = run(lambda o: shared + o, other)
    do_out(0)
    grad_rows = do_first(0, None)
    do_out_sum(1)
    start_out(2)
    do_bwd(2)
    grad_rows = do_first(1, grad_rows)
    do_out(1)
    groups = [(*ex[w][2:5], cots[w], cols[w]) for w in every]
    expert_g = run(lambda f: expert_grads(f, window_resolution, groups, experts), first)
    hidden = up_weight.shape[2]
    eg = ScatterSum(expert_g, (experts * hidden, experts * hidden), run)
    do_out_sum(2)
    out_rows = do_place(0, None)
    grad_rows = do_first(2, grad_rows)
    eg.add()
    groups = [(fwd[w][1], bwd[w][1], fwd[w][3], bwd[w][2]) for w in every]
    attn_g, col_sums = run(lambda r: attn_grads(r, groups), role)
    do_out(2)
    eg.add()
    ag = ScatterSum(attn_g, (4 * width,), run)
    out_rows = do_place(1, out_rows)
    ag.add()
    up_g, down_g = eg.finish()
    ag.add()

    totals = jnp.concatenate(
        [
            shared,
            small[2 * experts :],
            (sums[0] + sums[1] + sums[2])[:3],
            jnp.pad(col_sums[:1], ((0, 0), (0, model - 3 * width))),
        ],
        0,
    )
    totals = after(run.last, totals)
    for b in range(lax.axis_size("dp").bit_length() - 1):
        totals = totals + swap(totals, "dp", 1 << b)
    (attn_g,) = ag.finish()
    block = up_g.shape[0]
    grad_up = jnp.transpose(up_g.reshape(block, experts, hidden), (1, 0, 2))
    grad_down = jnp.transpose(down_g.reshape(block, experts, hidden), (1, 2, 0))
    grad_qkv = jnp.transpose(attn_g[:, : 3 * width].reshape(block, 3, width), (1, 0, 2))
    grad_out = attn_g[:, 3 * width :].T
    col = totals[4 * experts + 3]
    qv_grad = jnp.stack([col[:width], col[2 * width : 3 * width]]).reshape(qv_bias.shape)
    return (
        do_place(2, out_rows),
        grad_rows,
        totals[4 * experts],
        totals[4 * experts + 1],
        grad_qkv,
        qv_grad,
        grad_out,
        totals[4 * experts + 2],
        totals[:experts],
        totals[experts : 2 * experts],
        grad_up,
        totals[2 * experts : 3 * experts],
        grad_down,
        totals[3 * experts : 4 * experts],
    )


def solution(mesh):
    in_specs = (
        P("dp", None), P("dp", None), P("dp"), P("dp"), P("dp"), P(), P(),
        P(None, None, "tensor"), P(None, "tensor", None), P("tensor", None), P(), P(), P(),
        P(None, None, "tensor"), P(None, "tensor"), P(None, "tensor", None), P(),
    )
    out_specs = (
        P("dp", None), P("dp", None), P(), P(), P(None, "dp", "tensor"), P(None, "tensor", None),
        P("tensor", "dp"), P(), P(), P(), P(None, "dp", "tensor"), P(None, "tensor"),
        P(None, "tensor", "dp"), P(),
    )
    return jax.shard_map(body, mesh=mesh, in_specs=in_specs, out_specs=out_specs, check_vma=False)
```

```python
import functools
import math

import jax
import jax.numpy as jnp
from jax import lax
from jax.experimental import pallas as pl
from jax.experimental.pallas import tpu as pltpu
from jax.sharding import PartitionSpec as P

HEAD_DIM = 64
S = 768
TILE = 192
BACK = 656
ROLES = [[int(t in (0, 3)), int(t > 1), int(t < 2), t, t ^ 2, t ^ 1, t ^ 3] for t in range(4)]
EXPERT_MIB = 32
GRADS_MIB = 20
EPS = 1e-05
MASKED = -1000000000.0
SCALE = 1.0 / math.sqrt(HEAD_DIM)
F32 = jnp.float32
BF16 = jnp.bfloat16

NN = (((1,), (0,)), ((), ()))
NT = (((1,), (1,)), ((), ()))
TN = (((0,), (0,)), ((), ()))


def mm(a, b, dims=NN):
    return lax.dot_general(a, b, dims, preferred_element_type=F32)


def row_mean(v):
    lanes = 128
    total = v[:, 0:lanes]
    for i in range(1, v.shape[1] // lanes):
        total = total + v[:, i * lanes : (i + 1) * lanes]
    return jnp.sum(total, -1, keepdims=True) * (1.0 / v.shape[1])


def layer_norm(values):
    centred = values - row_mean(values)
    rstd = lax.rsqrt(row_mean(centred * centred) + EPS)
    return centred * rstd, rstd


def norm_back(scaled, xhat, rstd):
    return rstd * (scaled - row_mean(scaled) - xhat * row_mean(scaled * xhat))


def pick_rows(table_ref, expert):
    out = jnp.where(expert == 0, table_ref[0:1, :], table_ref[1:2, :])
    return jnp.where(expert == 2, table_ref[2:3, :], out)


def cost(flops=1e6):
    return pl.CostEstimate(flops=int(flops), bytes_accessed=1, transcendentals=0)


def window(w, n, rows=S):
    return pl.BlockSpec((rows, n), lambda i: (w, 0))


def full(a):
    return pl.BlockSpec(a.shape, lambda i: (0,) * a.ndim)


def params(mib):
    return pltpu.CompilerParams(vmem_limit_bytes=mib * 1024 * 1024)


def heads_forward(qkv_ref, cols_ref, mix_ref, lse_ref, base):
    width = qkv_ref.shape[0] // 3
    first = base // HEAD_DIM
    half = S // 2
    for h in range(width // HEAD_DIM):
        kt = qkv_ref[pl.ds(width + h * HEAD_DIM, HEAD_DIM), :]
        vt = qkv_ref[pl.ds(2 * width + h * HEAD_DIM, HEAD_DIM), :]
        k = kt.T
        for c in range(2):
            at = pl.ds(c * half, half)
            qt = qkv_ref[pl.ds(h * HEAD_DIM, HEAD_DIM), at]
            s = mm(k, qt) + cols_ref[:, c + 1 : c + 2]
            top = jnp.max(s, 0, keepdims=True)
            p = jnp.exp(s - top)
            total = jnp.sum(p, 0, keepdims=True)
            o = mm(vt, p.astype(BF16)) * (1.0 / total)
            mix_ref[pl.ds(base + h * HEAD_DIM, HEAD_DIM), at] = o.astype(BF16)
            lse_ref[pl.ds(first + h, 1), at] = top + jnp.log(total)


def project(wt_ref, wb_ref, normed, qkv_ref):
    width = wt_ref.shape[0] // 3
    bias = jnp.concatenate([wb_ref[...], jnp.zeros((6, width), F32)], 0).T
    for j in range(3):
        rows = pl.ds(j * width, width)
        part = mm(wt_ref[rows, :], normed, NT)
        if j != 1:
            part = part + bias[:, j // 2 : j // 2 + 1]
        part = part.astype(BF16)
        if j == 0:
            part = part * jnp.asarray(SCALE, BF16)
        qkv_ref[rows, :] = part


HBM = pl.BlockSpec(memory_space=pltpu.HBM)
SMEM = pl.BlockSpec(memory_space=pltpu.SMEM)
VMEM = pl.BlockSpec(memory_space=pltpu.VMEM)


def start(source, target, sem):
    copy = pltpu.make_async_copy(source, target, sem)
    copy.start()
    return copy


def attn_own_kernel(
    w, res_ref, x_ref, expert_ref, keep_ref, consts_ref, wt_ref, wb_ref, lse_ref, n1_ref, qkv_ref, mix_ref, cols_ref
):
    kind = lax.broadcasted_iota(jnp.int32, (8, S), 0)
    upper = lax.broadcasted_iota(jnp.int32, (8, S), 1) >= S // 2
    alike = jnp.logical_or(res_ref[w] > 0, upper == (kind == 2))
    seen = jnp.logical_and(keep_ref[w : w + 1, :] > 0, alike)
    facts = jnp.where(kind == 0, expert_ref[w : w + 1, :].astype(F32), jnp.where(seen, 0.0, MASKED))
    cols_ref[...] = facts.T
    xhat, _ = layer_norm(x_ref[...].astype(F32))
    n1_ref[...] = (xhat * consts_ref[0:1, :] + consts_ref[1:2, :]).astype(BF16)
    project(wt_ref, wb_ref, n1_ref[...], qkv_ref)
    heads_forward(qkv_ref, cols_ref, mix_ref, lse_ref, 0)


def attn_own(w, res, x, expert, keep, consts, wt, wb):
    rows, model = x.shape
    width = wt.shape[0] // 3
    return pl.pallas_call(
        functools.partial(attn_own_kernel, w),
        out_shape=(
            jax.ShapeDtypeStruct((width // HEAD_DIM, rows), F32),
            jax.ShapeDtypeStruct((rows, model), BF16),
            jax.ShapeDtypeStruct((3 * width, rows), BF16),
            jax.ShapeDtypeStruct((width, rows), BF16),
            jax.ShapeDtypeStruct((rows, 8), F32),
        ),
        in_specs=[SMEM] + [VMEM] * 6,
        out_specs=(VMEM,) * 5,
        compiler_params=params(9),
        cost_estimate=cost(),
        name="attn_own",
    )(res, x, expert, keep, consts, wt, wb)


def attn_comp_kernel(
    emit, role_ref, pieces, wt_ref, wo_ref, n1_ref, own_qkv_ref, own_ref, own_lse_ref, cols_ref, wb_ref,
    lse_ref, qkv_ref, mix_ref, *refs
):
    width = own_ref.shape[0]
    wide = 3 * width
    heads = width // HEAD_DIM
    if emit:
        wt_c_ref, wt_both_ref, wo_both_ref, wo_c_ref, pack_v = refs
        for j in range(4):
            at = pl.ds(pl.multiple_of(role_ref[7 + j] * width, width), width)
            pack_v[at, :] = pieces[j][...]
        wt_c_ref[...] = pack_v[0:wide, :]
        wo_both_ref[0:width, :] = wo_ref[...]
        wo_both_ref[width:, :] = pack_v[wide:, :]
        wo_c_ref[...] = pack_v[wide:, :]
        wt_both_ref[pl.ds(pl.multiple_of(role_ref[1] * wide, wide), wide), :] = wt_ref[...]
        wt_both_ref[pl.ds(pl.multiple_of(role_ref[2] * wide, wide), wide), :] = pack_v[0:wide, :]
        weights = wt_c_ref
    else:
        weights = wt_ref
    qkv_ref[0:wide, :] = own_qkv_ref[...]
    mix_ref[0:width, :] = own_ref[...]
    lse_ref[0:heads, :] = own_lse_ref[...]
    comp = qkv_ref.at[pl.ds(wide, wide), :]
    project(weights, wb_ref, n1_ref[...], comp)
    heads_forward(comp, cols_ref, mix_ref, lse_ref, width)


def attn_comp_first(role_ref, *refs):
    attn_comp_kernel(True, role_ref, refs[:4], *refs[4:])


def attn_comp(role, pieces, wt, wo, own, cols, wb):
    own_lse, n1, own_qkv, own_mix = own[:4]
    rows, model = n1.shape
    width = own_mix.shape[0]
    outs = (
        jax.ShapeDtypeStruct((2 * (width // HEAD_DIM), rows), F32),
        jax.ShapeDtypeStruct((6 * width, rows), BF16),
        jax.ShapeDtypeStruct((2 * width, rows), BF16),
        jax.ShapeDtypeStruct((3 * width, model), BF16),
        jax.ShapeDtypeStruct((6 * width, model), BF16),
        jax.ShapeDtypeStruct((2 * width, model), BF16),
        jax.ShapeDtypeStruct((width, model), BF16),
    )
    return pl.pallas_call(
        attn_comp_first,
        out_shape=outs,
        in_specs=[SMEM] + [VMEM] * 12,
        out_specs=(VMEM,) * len(outs),
        scratch_shapes=[pltpu.VMEM((4 * width, model), BF16)],
        compiler_params=params(9),
        cost_estimate=cost(),
        name="attn_comp",
    )(role, *pieces, wt, wo, n1, own_qkv, own_mix, own_lse, cols, wb)


def attn_both_kernel(
    w, res_ref, x_ref, expert_ref, keep_ref, consts_ref, wt_ref, wb_ref, wt_c_ref, wb_c_ref,
    lse_ref, n1_ref, qkv_ref, mix_ref, cols_ref,
):
    wide = wt_ref.shape[0]
    own = qkv_ref.at[pl.ds(0, wide), :]
    attn_own_kernel(
        w, res_ref, x_ref, expert_ref, keep_ref, consts_ref, wt_ref, wb_ref, lse_ref, n1_ref, own, mix_ref, cols_ref
    )
    comp = qkv_ref.at[pl.ds(wide, wide), :]
    project(wt_c_ref, wb_c_ref, n1_ref[...], comp)
    heads_forward(comp, cols_ref, mix_ref, lse_ref, wide // 3)


def attn_both(w, res, x, expert, keep, consts, wt, wb, wt_c, wb_c):
    rows, model = x.shape
    width = wt.shape[0] // 3
    return pl.pallas_call(
        functools.partial(attn_both_kernel, w),
        out_shape=(
            jax.ShapeDtypeStruct((2 * (width // HEAD_DIM), rows), F32),
            jax.ShapeDtypeStruct((rows, model), BF16),
            jax.ShapeDtypeStruct((6 * width, rows), BF16),
            jax.ShapeDtypeStruct((2 * width, rows), BF16),
            jax.ShapeDtypeStruct((rows, 8), F32),
        ),
        in_specs=[SMEM] + [VMEM] * 8,
        out_specs=(VMEM,) * 5,
        compiler_params=params(10),
        cost_estimate=cost(),
        name="attn_both",
    )(res, x, expert, keep, consts, wt, wb, wt_c, wb_c)


def present(first_ref, res_ref, w, tile, e):
    single = res_ref[w] > 0
    second = jnp.logical_and(jnp.logical_not(single), tile >= (S // TILE) // 2)
    image = first_ref[2 * w + second.astype(jnp.int32)]
    mixed = tile == S // TILE - 1
    mixed = jnp.logical_or(mixed, jnp.logical_and(jnp.logical_not(single), tile == (S // TILE) // 2 - 1))
    return jnp.logical_or(e == image, jnp.logical_and(mixed, e == 1))


def expert_kernel(
    w, role_ref, first_ref, res_ref, mix_ref, far_ref, wo_ref, wo_far_ref, wo_far_comp_ref, x_ref, cot_v,
    cols_ref, ob_ref, g2_ref, b2_ref, ub_ref, up_v, down_v,
    small_ref, mid_ref, n2_v, act_v, gpre_v, out_v, gn2_ref,
    mix_v, wo_v, xhat_v, gn2_v,
):
    experts = up_v.shape[0]
    width = mix_ref.shape[0] // 2
    tiles = S // TILE
    for j in range(4):
        at = pl.ds(pl.multiple_of(role_ref[3 + j] * width, width), width)
        piece = slice((j % 2) * width, (j % 2 + 1) * width)
        mix_v[at, :] = (mix_ref, far_ref)[j // 2][piece, :]
        wo_v[at, :] = wo_ref[piece, :] if j < 2 else (wo_far_ref, wo_far_comp_ref)[j - 2][...]
    expert = cols_ref[:, 0:1]
    small_ref[...] = jnp.zeros_like(small_ref)
    proj = mm(mix_v[...], wo_v[...], TN)
    middle = x_ref[...].astype(F32) + (proj + ob_ref[2:3, :])
    mid_ref[...] = middle.astype(BF16)
    xhat, _ = layer_norm(middle)
    xhat_v[...] = xhat
    n2_v[...] = (xhat * pick_rows(g2_ref, expert) + pick_rows(b2_ref, expert)).astype(BF16)

    def tile_step(tile, carry):
        at = pl.ds(pl.multiple_of(tile * TILE, TILE), TILE)
        for ref in (act_v, gpre_v, out_v, gn2_v):
            ref[at, :] = jnp.zeros((TILE, ref.shape[1]), BF16)

        def step(e, carry):
            @pl.when(present(first_ref, res_ref, w, tile, e))
            def _():
                mask = (cols_ref[at, 0:1] == e.astype(F32)).astype(F32)
                cot = cot_v[at, :]
                pre = mm(n2_v[at, :], up_v[e]) + ub_ref[pl.ds(e, 1), :]
                cdf = 0.5 + 0.5 * lax.erf(pre * (1.0 / math.sqrt(2.0)))
                act = (pre * cdf * mask).astype(BF16)
                slope = cdf + pre * (jnp.exp(-0.5 * pre * pre) * (1.0 / math.sqrt(2.0 * math.pi)))
                gpre = (mm(cot, down_v[e], NT) * slope * mask).astype(BF16)
                gn2 = mm(gpre, up_v[e], NT)
                out = mm(act, down_v[e])
                act_v[at, :] = act_v[at, :] + act
                gpre_v[at, :] = gpre_v[at, :] + gpre
                out_v[at, :] = out_v[at, :] + out.astype(BF16)
                gn2_v[at, :] = gn2_v[at, :] + gn2.astype(BF16)
                for j, values in enumerate(
                    (gn2 * xhat_v[at, :], gn2, gpre.astype(F32), cot.astype(F32) * mask)
                ):
                    row = pl.ds(j * experts + e, 1)
                    small_ref[row, :] = small_ref[row, :] + jnp.sum(values, 0, keepdims=True)

            return carry

        lax.fori_loop(0, experts, step, 0)
        return carry

    lax.fori_loop(0, tiles, tile_step, 0)
    gn2_ref[...] = gn2_v[0:BACK, :]


def expert_fwd_bwd(w, role, first, res, mix, far, wo, x, cot, cols, ob, g2, b2, ub, up, down):
    rows, model = x.shape
    experts, _, hidden = up.shape
    return pl.pallas_call(
        functools.partial(expert_kernel, w),
        out_shape=(
            jax.ShapeDtypeStruct((4 * experts, model), F32),
            jax.ShapeDtypeStruct((rows, model), BF16),
            jax.ShapeDtypeStruct((rows, model), BF16),
            jax.ShapeDtypeStruct((rows, hidden), BF16),
            jax.ShapeDtypeStruct((rows, hidden), BF16),
            jax.ShapeDtypeStruct((rows, model), BF16),
            jax.ShapeDtypeStruct((BACK, model), BF16),
        ),
        in_specs=[SMEM] * 3 + [VMEM] * 14,
        out_specs=(VMEM,) * 7,
        scratch_shapes=[
            pltpu.VMEM((rows, model), BF16),
            pltpu.VMEM((rows, model), BF16),
            pltpu.VMEM((rows, model), F32),
            pltpu.VMEM((rows, model), BF16),
        ],
        compiler_params=params(22),
        cost_estimate=cost(1e11),
        name="expert_fwd_bwd",
    )(role, first, res, mix, far, *wo, x, cot, cols, ob, g2, b2, ub, up, down)


def expert_grads_kernel(windows, first_ref, res_ref, *refs):
    groups = [refs[5 * w : 5 * w + 5] for w in range(windows)]
    out_ref, acc = refs[-2:]
    e, kind = pl.program_id(0), pl.program_id(1)
    tiles = S // TILE
    acc[...] = jnp.zeros_like(acc)

    def add(cols_ref, row, count, left, right):
        at = pl.ds(pl.multiple_of(row, TILE), count)
        mask = (cols_ref[at, 0:1] == e.astype(F32)).astype(BF16)
        acc[...] += mm(left[at, :], right[at, :] * mask, TN)

    def half_step(w, half, carry):
        n2_ref, act_ref, gpre_ref, cot_ref, cols_ref = groups[w]
        tile = 2 * half
        row = tile * TILE
        here = present(first_ref, res_ref, w, tile, e)
        next_ = present(first_ref, res_ref, w, tile + 1, e)
        for k, (left, right) in enumerate(((n2_ref, gpre_ref), (cot_ref, act_ref))):

            @pl.when(jnp.logical_and(kind == k, jnp.logical_and(here, next_)))
            def _():
                add(cols_ref, row, 2 * TILE, left, right)

            @pl.when(jnp.logical_and(kind == k, here != next_))
            def _():
                add(cols_ref, row + jnp.where(here, 0, TILE), TILE, left, right)

        return carry

    for w in range(windows):
        lax.fori_loop(0, tiles // 2, functools.partial(half_step, w), 0)
    out_ref[...] = acc[...].astype(BF16)


def expert_grads(first, res, groups, experts):
    model = groups[0][0].shape[1]
    hidden = groups[0][1].shape[1]
    flat = [a for g in groups for a in g]
    return pl.pallas_call(
        functools.partial(expert_grads_kernel, len(groups)),
        grid=(experts, 2),
        out_shape=jax.ShapeDtypeStruct((model, 2 * experts * hidden), BF16),
        in_specs=[SMEM] * 2 + [VMEM] * len(flat),
        out_specs=pl.BlockSpec((model, hidden), lambda e, k: (0, k * experts + e)),
        scratch_shapes=[pltpu.VMEM((model, hidden), F32)],
        compiler_params=params(9),
        cost_estimate=cost(1e11),
        name="expert_grads",
    )(first, res, *flat)


def mid_back_kernel(s_ref, r_ref, mid_ref, cot_ref, cols_ref, g2_ref, ga_ref):
    top = slice(0, BACK)
    total = s_ref[...].astype(F32) + r_ref[...].astype(F32)
    xhat, rstd = layer_norm(mid_ref[top, :].astype(F32))
    gain = pick_rows(g2_ref, cols_ref[top, 0:1])
    grad = cot_ref[top, :].astype(F32) + norm_back(total * gain, xhat, rstd)
    ga_ref[...] = grad.astype(BF16)


def mid_back(s, r, mid, cot, cols, g2):
    return pl.pallas_call(
        mid_back_kernel,
        out_shape=jax.ShapeDtypeStruct(s.shape, BF16),
        in_specs=[VMEM] * 6,
        out_specs=VMEM,
        compiler_params=params(10),
        cost_estimate=cost(1e11),
        name="mid_back",
    )(s, r, mid, cot, cols, g2)


def attn_bwd_kernel(
    role_ref, ga_ref, far_ref, cols_ref, wt_ref, wo_ref, mix_ref, qkv_ref, lse_ref,
    gn1_ref, dqkv_ref, gaf_ref, gmt_v,
):
    width = wo_ref.shape[0] // 2
    wide = 3 * width
    heads = width // HEAD_DIM
    take = role_ref[0] > 0
    top = pl.ds(0, BACK)

    @pl.when(take)
    def _():
        gaf_ref[top, :] = far_ref[...]

    @pl.when(jnp.logical_not(take))
    def _():
        gaf_ref[top, :] = ga_ref[...]

    gaf_ref[BACK:, :] = jnp.zeros((S - BACK, gaf_ref.shape[1]), BF16)
    gmt_v[...] = mm(wo_ref[...], gaf_ref[...], NT).astype(BF16)
    half = S // 2

    def group(g, carry):
        into = role_ref[1 + g] * wide
        for h in range(heads):
            at = lambda base, step: pl.ds(pl.multiple_of(base + h * HEAD_DIM, HEAD_DIM), HEAD_DIM)
            both = at(g * width, 0)
            q_rows, k_rows, v_rows = (at(g * wide + j * width, 0) for j in range(3))
            q_into, k_into, v_into = (at(into + j * width, 0) for j in range(3))
            kt, vt = qkv_ref[k_rows, :], qkv_ref[v_rows, :]
            k, v = kt.T, vt.T
            row = pl.ds(g * heads + h, 1)
            dk = dv = None
            for c in range(2):
                part = pl.ds(c * half, half)
                qt = qkv_ref[q_rows, part]
                dot = gmt_v[both, part]
                delta = jnp.sum(dot.astype(F32) * mix_ref[both, part].astype(F32), 0, keepdims=True)
                s = mm(k, qt) + cols_ref[:, c + 1 : c + 2]
                p = jnp.exp(s - lse_ref[row, part])
                ds = (p * (mm(v, dot) - delta)).astype(BF16)
                dv_c = mm(p.astype(BF16), dot, NT)
                dk_c = mm(ds, qt, NT)
                dv = dv_c if dv is None else dv + dv_c
                dk = dk_c if dk is None else dk + dk_c
                dqkv_ref[q_into, part] = (mm(kt, ds) * SCALE).astype(BF16)
            dqkv_ref[k_into, :] = dk.astype(BF16).T
            dqkv_ref[v_into, :] = dv.astype(BF16).T
        return carry

    lax.fori_loop(0, 2, group, 0)
    gn1_ref[...] = mm(dqkv_ref[:, 0:BACK], wt_ref[...], TN).astype(BF16)


def attn_bwd(role, ga, far, cols, wt, wo, mix, qkv, lse):
    model = wo.shape[1]
    return pl.pallas_call(
        attn_bwd_kernel,
        out_shape=(
            jax.ShapeDtypeStruct((BACK, model), BF16),
            jax.ShapeDtypeStruct(qkv.shape, BF16),
            jax.ShapeDtypeStruct((S, model), BF16),
        ),
        in_specs=[SMEM] + [VMEM] * 8,
        out_specs=(VMEM,) * 3,
        scratch_shapes=[pltpu.VMEM(mix.shape, BF16)],
        compiler_params=params(11),
        cost_estimate=cost(1e11),
        name="attn_bwd",
    )(role, ga, far, cols, wt, wo, mix, qkv, lse)


def attn_grads_kernel(role_ref, *refs):
    windows = (len(refs) - 8) // 4
    groups = [refs[4 * w : 4 * w + 4] for w in range(windows)]
    out_ref, sum_ref, n1_v, gaf_v, dqkv_v, mix_v, acc, sems = refs[-8:]
    wide = dqkv_v.shape[0]
    own = pl.ds(pl.multiple_of(role_ref[1] * wide, wide), wide)
    loads = []
    for w, (n1_ref, dqkv_ref, mix_ref, gaf_ref) in enumerate(groups):
        at = pl.ds(w * S, S)
        pairs = (
            (dqkv_ref.at[own, :], dqkv_v.at[:, at]),
            (n1_ref, n1_v.at[at, :]),
            (mix_ref.at[pl.ds(0, mix_v.shape[0]), :], mix_v.at[:, at]),
            (gaf_ref, gaf_v.at[at, :]),
        )
        loads += [start(a, b, sems.at[4 * w + j]) for j, (a, b) in enumerate(pairs)]
    for load in loads:
        load.wait()
    acc[0:wide, :] = mm(dqkv_v[...], n1_v[...])
    acc[wide:, :] = mm(mix_v[...], gaf_v[...])
    sum_ref[...] = mm(jnp.ones((8, dqkv_v.shape[1]), BF16), dqkv_v[...], NT)
    out_ref[...] = acc[...].astype(BF16).T


def attn_grads(role, groups):
    n1, dqkv = groups[0][:2]
    model = n1.shape[1]
    wide = dqkv.shape[0] // 2
    rows = len(groups) * S
    flat = [a for g in groups for a in g]
    outs = (
        jax.ShapeDtypeStruct((model, wide + wide // 3), BF16),
        jax.ShapeDtypeStruct((8, wide), F32),
    )
    return pl.pallas_call(
        attn_grads_kernel,
        grid=(1,),
        out_shape=outs,
        in_specs=[SMEM] + [HBM] * len(flat),
        out_specs=tuple(full(o) for o in outs),
        scratch_shapes=[
            pltpu.VMEM((rows, model), BF16),
            pltpu.VMEM((rows, model), BF16),
            pltpu.VMEM((wide, rows), BF16),
            pltpu.VMEM((wide // 3, rows), BF16),
            pltpu.VMEM((wide + wide // 3, model), F32),
            pltpu.SemaphoreType.DMA((4 * len(groups),)),
        ],
        compiler_params=params(50),
        cost_estimate=cost(1e11),
        name="attn_grads",
    )(role, *flat)


def first_back_kernel(w, s_ref, r_ref, ga_ref, x_ref, g_ref, *refs):
    out_ref, sum_ref, out_v, sem = refs[-4:]
    top = slice(0, BACK)
    total = s_ref[...].astype(F32) + r_ref[...].astype(F32)
    xhat, rstd = layer_norm(x_ref[top, :].astype(F32))
    ga = ga_ref[top, :].astype(F32)
    back = norm_back(total * g_ref[0:1, :], xhat, rstd)
    out_v[top, :] = (ga + back).astype(BF16)
    out_v[BACK:, :] = jnp.zeros((S - BACK, out_v.shape[1]), BF16)
    copy = start(out_v, out_ref.at[pl.ds(w * S, S), :], sem)
    sum_ref[...] = jnp.zeros_like(sum_ref)
    for j, values in enumerate((total * xhat, total, ga)):
        sum_ref[j : j + 1, :] = jnp.sum(values, 0, keepdims=True)
    copy.wait()


def first_back(w, s, r, ga, x, g, rows, into):
    model = s.shape[1]
    more = () if into is None else (into,)
    return pl.pallas_call(
        functools.partial(first_back_kernel, w),
        out_shape=(
            jax.ShapeDtypeStruct((rows, model), BF16),
            jax.ShapeDtypeStruct((8, model), F32),
        ),
        in_specs=[VMEM] * 5 + [HBM] * len(more),
        out_specs=(HBM, VMEM),
        scratch_shapes=[pltpu.VMEM((S, model), BF16), pltpu.SemaphoreType.DMA],
        input_output_aliases={5: 0} if more else {},
        compiler_params=params(12),
        cost_estimate=cost(1e11),
        name="first_back",
    )(s, r, ga, x, g, *more)


def layer_out_kernel(s_ref, r_ref, mid_ref, cols_ref, db_ref, out_ref):
    total = s_ref[...].astype(F32) + r_ref[...].astype(F32)
    shift = pick_rows(db_ref, cols_ref[:, 0:1])
    out_ref[...] = (mid_ref[...].astype(F32) + (total + shift)).astype(BF16)


def layer_out_rows(s, r, mid, cols, db):
    return pl.pallas_call(
        layer_out_kernel,
        out_shape=jax.ShapeDtypeStruct(mid.shape, BF16),
        in_specs=[VMEM] * 5,
        out_specs=VMEM,
        compiler_params=params(10),
        cost_estimate=cost(1e11),
        name="layer_out_rows",
    )(s, r, mid, cols, db)


def place_kernel(w, role_ref, own_ref, far_ref, *refs):
    out_ref, out_v, sem = refs[-3:]

    @pl.when(role_ref[0] > 0)
    def _():
        out_v[...] = far_ref[...]

    @pl.when(role_ref[0] == 0)
    def _():
        out_v[...] = own_ref[...]

    start(out_v, out_ref.at[pl.ds(w * S, S), :], sem).wait()


def place_rows(w, role, own, far, rows, into):
    model = own.shape[1]
    more = () if into is None else (into,)
    return pl.pallas_call(
        functools.partial(place_kernel, w),
        out_shape=jax.ShapeDtypeStruct((rows, model), BF16),
        in_specs=[SMEM] + [VMEM] * 2 + [HBM] * len(more),
        out_specs=HBM,
        scratch_shapes=[pltpu.VMEM((S, model), BF16), pltpu.SemaphoreType.DMA],
        input_output_aliases={3: 0} if more else {},
        compiler_params=params(5),
        cost_estimate=cost(1e11),
        name="place_rows",
    )(role, own, far, *more)


def inward(v):
    return lax.ppermute(v, "tensor", [(0, 1), (3, 2)])


def across(v):
    return lax.ppermute(v, "tensor", [(1, 2), (2, 1)])


def outward(v):
    return lax.ppermute(v, "tensor", [(1, 0), (2, 3)])


def swap(v, axis, bit):
    return lax.ppermute(v, axis, [(i, i ^ bit) for i in range(lax.axis_size(axis))])


def add_rounded(a, b):
    return (a.astype(F32) + b.astype(F32)).astype(BF16)


def after(first, value):
    return lax.optimization_barrier((first, value))[1]


class Order:
    def __init__(self):
        self.last = None

    def __call__(self, step, value, *rest):
        if self.last is not None:
            value = after(self.last, value)
        out = step(value, *rest)
        leaves = jax.tree.leaves(out)
        self.last = min(leaves, key=lambda a: a.size)
        return out


def halve(value, left, bit, run):
    axis, mine = left.index(bit), (lax.axis_index("dp") >> bit) & 1
    sent = run(lambda v: lax.dynamic_index_in_dim(v, 1 - mine, axis, keepdims=False), value)
    got = swap(sent, "dp", 1 << bit)

    def add(got, value):
        return add_rounded(lax.dynamic_index_in_dim(value, mine, axis, keepdims=False), got)

    return value, got, add, [b for b in left if b != bit]


class ScatterSum:
    def __init__(self, value, widths, run):
        self.run, self.widths = run, widths
        count = lax.axis_size("dp")
        bits = count.bit_length() - 1
        rows, columns = value.shape
        value = value.reshape((2,) * bits + (rows // count, columns))
        self.parts = [(halve(value, list(range(bits - 1, -1, -1)), 0, run), 1)]

    def add(self):
        values = [(self.run(h[2], h[1], h[0]), h[3], way) for h, way in self.parts]
        if self.widths:
            value, left, _ = values[0]
            ends = [sum(self.widths[: k + 1]) for k in range(len(self.widths))]
            values = [
                (value[..., e - n : e], left, (-1) ** k)
                for k, (e, n) in enumerate(zip(ends, self.widths))
            ]
            self.widths = None
        if not values[0][1]:
            return [v.astype(F32) for v, _, _ in values]
        self.parts = [
            (halve(v, left, left[::-way][0], self.run), way) for v, left, way in values
        ]
        return None

    def finish(self):
        done = None
        while done is None:
            done = self.add()
        return done


def body(
    inputs, cotangent, row_expert, row_keep, window_resolution, attention_norm_gain,
    attention_norm_bias, qkv_weight, qv_bias, out_weight, out_bias, second_gain,
    expert_norm_bias, up_weight, up_bias, down_weight, down_bias,
):
    row_count, model = inputs.shape
    experts = up_weight.shape[0]
    width = qkv_weight.shape[2]
    windows = row_count // S
    tiles = S // TILE
    me = lax.axis_index("tensor")
    low = me < 2
    at_end = (me == 0) | (me == 3)
    place = lax.axis_index("dp")
    turn = ((place >> 1) & 1) + 2 * (place & 1)
    role = jnp.concatenate(
        [
            jnp.asarray(ROLES, jnp.int32)[me],
            turn ^ jnp.arange(4, dtype=jnp.int32),
        ]
    )
    run = Order()

    wt = jnp.transpose(qkv_weight, (0, 2, 1)).reshape(3 * width, model)
    pack = jnp.concatenate([wt, out_weight], 0)
    part = lax.dynamic_slice_in_dim(pack, turn * width, width, 0)
    part = swap(part, "tensor", 2)
    wo_far = swap(out_weight, "tensor", 1)
    wb = qv_bias.reshape(2, width)
    wb_c = swap(wb, "tensor", 2)
    every = range(windows)
    expert_rows, keep_rows = row_expert.reshape(windows, S), row_keep.reshape(windows, S)
    consts = jnp.stack([attention_norm_gain, attention_norm_bias, out_bias])
    at = [slice(w * S, (w + 1) * S) for w in every]
    xs, cots = [inputs[at[0]], None, None], [None] * windows

    given = (expert_rows, keep_rows, consts, wt, wb)
    own_lse, n1, own_qkv, own_mix, facts = run(
        lambda x: attn_own(0, window_resolution, x, *given), xs[0]
    )
    part = after(wo_far, after(wb_c, after(run.last, part)))
    beside = swap(part, "dp", 2)
    across_core = swap(part, "dp", 1)
    for w in every:
        cots[w] = run(lambda c: c[at[w]], cotangent)
    first = run(lambda e: e[:: S // 2], row_expert)
    beside = after(run.last, beside)
    last = swap(beside, "dp", 1)
    for w in (1, 2):
        xs[w] = run(lambda c: c[at[w]], inputs)
    lse, qkv, mix, wt_c, wt_both, wo_both, wo_c = run(
        lambda f: attn_comp(
            role, (part, beside, across_core, f), wt, out_weight, (own_lse, n1, own_qkv, own_mix), facts, wb_c
        ),
        last,
    )
    wo = (wo_both, wo_far, swap(wo_c, "tensor", 1))
    fwd = [(lse, n1, qkv, mix, facts)]
    mix_far = [swap(mix, "tensor", 1)]
    for w in (1, 2):
        fwd.append(run(lambda x: attn_both(w, window_resolution, x, *given, wt_c, wb_c), xs[w]))
        mix_far.append(swap(fwd[w][3], "tensor", 1))
    cols = [fwd[w][4] for w in every]

    ex, gn2_in, s2, ga, bwd = ([None] * windows for _ in range(5))
    part_in, s_out, lo, sums = ([None] * windows for _ in range(4))

    def do_experts(w):
        def step(far_mix):
            return expert_fwd_bwd(
                w, role, first, window_resolution, fwd[w][3], far_mix, wo, xs[w],
                cots[w], cols[w], consts, second_gain, expert_norm_bias, up_bias, up_weight, down_weight,
            )

        ex[w] = run(step, mix_far[w])
        gn2_in[w] = inward(ex[w][6])

    def do_sum2(w):
        s2[w] = run(add_rounded, gn2_in[w], ex[w][6])

    def do_mid(w):
        ga[w] = run(
            lambda r: mid_back(s2[w], r, ex[w][1], cots[w], cols[w], second_gain), across(s2[w])
        )

    def do_bwd(w):
        lse, _, qkv, mix, _ = fwd[w]
        bwd[w] = run(
            lambda far: attn_bwd(role, ga[w], far, cols[w], wt_both, wo_both, mix, qkv, lse),
            outward(ga[w]),
        )

    def do_first(w, into):
        gn1, _, gaf = bwd[w]
        into, sums[w] = run(
            lambda r: first_back(w, gn1, r, gaf, xs[w], consts, row_count, into),
            swap(gn1, "tensor", 1),
        )
        return into

    def do_place(w, into):
        return run(lambda f: place_rows(w, role, lo[w], f, row_count, into), outward(lo[w]))

    def start_out(w):
        part_in[w] = inward(after(run.last, ex[w][5]))

    def do_out_sum(w):
        s_out[w] = run(add_rounded, part_in[w], ex[w][5])

    def do_out(w):
        lo[w] = run(
            lambda r: layer_out_rows(s_out[w], r, ex[w][1], cols[w], down_bias), across(s_out[w])
        )

    do_experts(0)
    do_experts(1)
    do_sum2(0)
    do_experts(2)
    start_out(0)
    small = run(lambda a, b, c: a + b + c, ex[2][0], ex[0][0], ex[1][0])
    shared = small[: 2 * experts]
    other = swap(shared, "tensor", 1)
    do_sum2(1)
    do_mid(0)
    do_sum2(2)
    do_mid(1)
    do_bwd(0)
    shared = run(lambda o: shared + o, other)
    other = swap(shared, "tensor", 2)
    start_out(1)
    do_out_sum(0)
    do_mid(2)
    do_bwd(1)
    shared = run(lambda o: shared + o, other)
    do_out(0)
    grad_rows = do_first(0, None)
    do_out_sum(1)
    start_out(2)
    do_bwd(2)
    grad_rows = do_first(1, grad_rows)
    do_out(1)
    groups = [(*ex[w][2:5], cots[w], cols[w]) for w in every]
    expert_g = run(lambda f: expert_grads(f, window_resolution, groups, experts), first)
    hidden = up_weight.shape[2]
    eg = ScatterSum(expert_g, (experts * hidden, experts * hidden), run)
    do_out_sum(2)
    out_rows = do_place(0, None)
    eg.add()
    grad_rows = do_first(2, grad_rows)
    groups = [(fwd[w][1], bwd[w][1], fwd[w][3], bwd[w][2]) for w in every]
    attn_g, col_sums = run(lambda r: attn_grads(r, groups), role)
    do_out(2)
    eg.add()
    ag = ScatterSum(attn_g, (4 * width,), run)
    out_rows = do_place(1, out_rows)
    ag.add()
    up_g, down_g = eg.finish()
    ag.add()
    totals = jnp.concatenate(
        [
            shared,
            small[2 * experts :],
            (sums[0] + sums[1] + sums[2])[:3],
            jnp.pad(col_sums[:1], ((0, 0), (0, model - 3 * width))),
        ],
        0,
    )
    totals = after(run.last, totals)
    for b in range(lax.axis_size("dp").bit_length() - 1):
        totals = totals + swap(totals, "dp", 1 << b)
    (attn_g,) = ag.finish()
    block = up_g.shape[0]
    grad_up = jnp.transpose(up_g.reshape(block, experts, hidden), (1, 0, 2))
    grad_down = jnp.transpose(down_g.reshape(block, experts, hidden), (1, 2, 0))
    grad_qkv = jnp.transpose(attn_g[:, : 3 * width].reshape(block, 3, width), (1, 0, 2))
    grad_out = attn_g[:, 3 * width :].T
    col = totals[4 * experts + 3]
    qv_grad = jnp.stack([col[:width], col[2 * width : 3 * width]]).reshape(qv_bias.shape)
    return (
        do_place(2, out_rows),
        grad_rows,
        totals[4 * experts],
        totals[4 * experts + 1],
        grad_qkv,
        qv_grad,
        grad_out,
        totals[4 * experts + 2],
        totals[:experts],
        totals[experts : 2 * experts],
        grad_up,
        totals[2 * experts : 3 * experts],
        grad_down,
        totals[3 * experts : 4 * experts],
    )


def solution(mesh):
    in_specs = (
        P("dp", None), P("dp", None), P("dp"), P("dp"), P("dp"), P(), P(),
        P(None, None, "tensor"), P(None, "tensor", None), P("tensor", None), P(), P(), P(),
        P(None, None, "tensor"), P(None, "tensor"), P(None, "tensor", None), P(),
    )
    out_specs = (
        P("dp", None), P("dp", None), P(), P(), P(None, "dp", "tensor"), P(None, "tensor", None),
        P("tensor", "dp"), P(), P(), P(), P(None, "dp", "tensor"), P(None, "tensor"),
        P(None, "tensor", "dp"), P(),
    )
    return jax.shard_map(body, mesh=mesh, in_specs=in_specs, out_specs=out_specs, check_vma=False)
```

```python
import functools
import math

import jax
import jax.numpy as jnp
from jax import lax
from jax.experimental import pallas as pl
from jax.experimental.pallas import tpu as pltpu
from jax.sharding import PartitionSpec as P

HEAD_DIM = 64
S = 768
TILE = 192
BACK = 656
ROLES = [[int(t in (0, 3)), int(t > 1), int(t < 2), t, t ^ 2, t ^ 1, t ^ 3] for t in range(4)]
EXPERT_MIB = 32
GRADS_MIB = 20
EPS = 1e-05
MASKED = -1000000000.0
SCALE = 1.0 / math.sqrt(HEAD_DIM)
F32 = jnp.float32
BF16 = jnp.bfloat16

NN = (((1,), (0,)), ((), ()))
NT = (((1,), (1,)), ((), ()))
TN = (((0,), (0,)), ((), ()))


def mm(a, b, dims=NN):
    return lax.dot_general(a, b, dims, preferred_element_type=F32)


def row_mean(v):
    lanes = 128
    total = v[:, 0:lanes]
    for i in range(1, v.shape[1] // lanes):
        total = total + v[:, i * lanes : (i + 1) * lanes]
    return jnp.sum(total, -1, keepdims=True) * (1.0 / v.shape[1])


def layer_norm(values):
    centred = values - row_mean(values)
    rstd = lax.rsqrt(row_mean(centred * centred) + EPS)
    return centred * rstd, rstd


def norm_back(scaled, xhat, rstd):
    return rstd * (scaled - row_mean(scaled) - xhat * row_mean(scaled * xhat))


def pick_rows(table_ref, expert):
    out = jnp.where(expert == 0, table_ref[0:1, :], table_ref[1:2, :])
    return jnp.where(expert == 2, table_ref[2:3, :], out)


def cost(flops=1e6):
    return pl.CostEstimate(flops=int(flops), bytes_accessed=1, transcendentals=0)


def window(w, n, rows=S):
    return pl.BlockSpec((rows, n), lambda i: (w, 0))


def full(a):
    return pl.BlockSpec(a.shape, lambda i: (0,) * a.ndim)


def params(mib):
    return pltpu.CompilerParams(vmem_limit_bytes=mib * 1024 * 1024)


def heads_forward(qkv_ref, cols_ref, mix_ref, lse_ref, base):
    width = qkv_ref.shape[0] // 3
    half = S // 2

    def head(h, carry):
        rows = lambda first: pl.ds(pl.multiple_of(first + h * HEAD_DIM, HEAD_DIM), HEAD_DIM)
        kt, vt = qkv_ref[rows(width), :], qkv_ref[rows(2 * width), :]
        k = kt.T
        for c in range(2):
            at = pl.ds(c * half, half)
            s = mm(k, qkv_ref[rows(0), at]) + cols_ref[:, c + 1 : c + 2]
            top = jnp.max(s, 0, keepdims=True)
            p = jnp.exp(s - top)
            total = jnp.sum(p, 0, keepdims=True)
            o = mm(vt, p.astype(BF16)) * (1.0 / total)
            mix_ref[rows(base), at] = o.astype(BF16)
            lse_ref[pl.ds(base // HEAD_DIM + h, 1), at] = top + jnp.log(total)
        return carry

    lax.fori_loop(0, width // HEAD_DIM, head, 0)


def project(wt_ref, wb_ref, normed, qkv_ref):
    width = wt_ref.shape[0] // 3
    bias = jnp.concatenate([wb_ref[...], jnp.zeros((6, width), F32)], 0).T
    for j in range(3):
        rows = pl.ds(j * width, width)
        part = mm(wt_ref[rows, :], normed, NT)
        if j != 1:
            part = part + bias[:, j // 2 : j // 2 + 1]
        part = part.astype(BF16)
        if j == 0:
            part = part * jnp.asarray(SCALE, BF16)
        qkv_ref[rows, :] = part


HBM = pl.BlockSpec(memory_space=pltpu.HBM)
SMEM = pl.BlockSpec(memory_space=pltpu.SMEM)
VMEM = pl.BlockSpec(memory_space=pltpu.VMEM)


def start(source, target, sem):
    copy = pltpu.make_async_copy(source, target, sem)
    copy.start()
    return copy


def attn_own_kernel(
    w, res_ref, x_ref, expert_ref, keep_ref, consts_ref, wt_ref, wb_ref, lse_ref, n1_ref, qkv_ref, mix_ref, cols_ref
):
    kind = lax.broadcasted_iota(jnp.int32, (8, S), 0)
    upper = lax.broadcasted_iota(jnp.int32, (8, S), 1) >= S // 2
    alike = jnp.logical_or(res_ref[w] > 0, upper == (kind == 2))
    seen = jnp.logical_and(keep_ref[w : w + 1, :] > 0, alike)
    facts = jnp.where(kind == 0, expert_ref[w : w + 1, :].astype(F32), jnp.where(seen, 0.0, MASKED))
    cols_ref[...] = facts.T
    xhat, _ = layer_norm(x_ref[...].astype(F32))
    n1_ref[...] = (xhat * consts_ref[0:1, :] + consts_ref[1:2, :]).astype(BF16)
    project(wt_ref, wb_ref, n1_ref[...], qkv_ref)
    heads_forward(qkv_ref, cols_ref, mix_ref, lse_ref, 0)


def attn_own(w, res, x, expert, keep, consts, wt, wb):
    rows, model = x.shape
    width = wt.shape[0] // 3
    return pl.pallas_call(
        functools.partial(attn_own_kernel, w),
        out_shape=(
            jax.ShapeDtypeStruct((width // HEAD_DIM, rows), F32),
            jax.ShapeDtypeStruct((rows, model), BF16),
            jax.ShapeDtypeStruct((3 * width, rows), BF16),
            jax.ShapeDtypeStruct((width, rows), BF16),
            jax.ShapeDtypeStruct((rows, 8), F32),
        ),
        in_specs=[SMEM] + [VMEM] * 6,
        out_specs=(VMEM,) * 5,
        compiler_params=params(9),
        cost_estimate=cost(),
        name="attn_own",
    )(res, x, expert, keep, consts, wt, wb)


def attn_comp_kernel(
    emit, role_ref, pieces, wt_ref, wo_ref, n1_ref, own_qkv_ref, own_ref, own_lse_ref, cols_ref, wb_ref,
    lse_ref, qkv_ref, mix_ref, *refs
):
    width = own_ref.shape[0]
    wide = 3 * width
    heads = width // HEAD_DIM
    if emit:
        wt_c_ref, wt_both_ref, wo_both_ref, wo_c_ref, pack_v = refs
        for j in range(4):
            at = pl.ds(pl.multiple_of(role_ref[7 + j] * width, width), width)
            pack_v[at, :] = pieces[j][...]
        wt_c_ref[...] = pack_v[0:wide, :]
        wo_both_ref[0:width, :] = wo_ref[...]
        wo_both_ref[width:, :] = pack_v[wide:, :]
        wo_c_ref[...] = pack_v[wide:, :]
        wt_both_ref[pl.ds(pl.multiple_of(role_ref[1] * wide, wide), wide), :] = wt_ref[...]
        wt_both_ref[pl.ds(pl.multiple_of(role_ref[2] * wide, wide), wide), :] = pack_v[0:wide, :]
        weights = wt_c_ref
    else:
        weights = wt_ref
    qkv_ref[0:wide, :] = own_qkv_ref[...]
    mix_ref[0:width, :] = own_ref[...]
    lse_ref[0:heads, :] = own_lse_ref[...]
    comp = qkv_ref.at[pl.ds(wide, wide), :]
    project(weights, wb_ref, n1_ref[...], comp)
    heads_forward(comp, cols_ref, mix_ref, lse_ref, width)


def attn_comp_first(role_ref, *refs):
    attn_comp_kernel(True, role_ref, refs[:4], *refs[4:])


def attn_comp(role, pieces, wt, wo, own, cols, wb):
    own_lse, n1, own_qkv, own_mix = own[:4]
    rows, model = n1.shape
    width = own_mix.shape[0]
    outs = (
        jax.ShapeDtypeStruct((2 * (width // HEAD_DIM), rows), F32),
        jax.ShapeDtypeStruct((6 * width, rows), BF16),
        jax.ShapeDtypeStruct((2 * width, rows), BF16),
        jax.ShapeDtypeStruct((3 * width, model), BF16),
        jax.ShapeDtypeStruct((6 * width, model), BF16),
        jax.ShapeDtypeStruct((2 * width, model), BF16),
        jax.ShapeDtypeStruct((width, model), BF16),
    )
    return pl.pallas_call(
        attn_comp_first,
        out_shape=outs,
        in_specs=[SMEM] + [VMEM] * 12,
        out_specs=(VMEM,) * len(outs),
        scratch_shapes=[pltpu.VMEM((4 * width, model), BF16)],
        compiler_params=params(9),
        cost_estimate=cost(),
        name="attn_comp",
    )(role, *pieces, wt, wo, n1, own_qkv, own_mix, own_lse, cols, wb)


def attn_both_kernel(
    w, res_ref, x_ref, expert_ref, keep_ref, consts_ref, wt_ref, wb_ref, wt_c_ref, wb_c_ref,
    lse_ref, n1_ref, qkv_ref, mix_ref, cols_ref,
):
    wide = wt_ref.shape[0]
    own = qkv_ref.at[pl.ds(0, wide), :]
    attn_own_kernel(
        w, res_ref, x_ref, expert_ref, keep_ref, consts_ref, wt_ref, wb_ref, lse_ref, n1_ref, own, mix_ref, cols_ref
    )
    comp = qkv_ref.at[pl.ds(wide, wide), :]
    project(wt_c_ref, wb_c_ref, n1_ref[...], comp)
    heads_forward(comp, cols_ref, mix_ref, lse_ref, wide // 3)


def attn_both(w, res, x, expert, keep, consts, wt, wb, wt_c, wb_c):
    rows, model = x.shape
    width = wt.shape[0] // 3
    return pl.pallas_call(
        functools.partial(attn_both_kernel, w),
        out_shape=(
            jax.ShapeDtypeStruct((2 * (width // HEAD_DIM), rows), F32),
            jax.ShapeDtypeStruct((rows, model), BF16),
            jax.ShapeDtypeStruct((6 * width, rows), BF16),
            jax.ShapeDtypeStruct((2 * width, rows), BF16),
            jax.ShapeDtypeStruct((rows, 8), F32),
        ),
        in_specs=[SMEM] + [VMEM] * 8,
        out_specs=(VMEM,) * 5,
        compiler_params=params(10),
        cost_estimate=cost(),
        name="attn_both",
    )(res, x, expert, keep, consts, wt, wb, wt_c, wb_c)


def present(first_ref, res_ref, w, tile, e):
    single = res_ref[w] > 0
    second = jnp.logical_and(jnp.logical_not(single), tile >= (S // TILE) // 2)
    image = first_ref[2 * w + second.astype(jnp.int32)]
    mixed = tile == S // TILE - 1
    mixed = jnp.logical_or(mixed, jnp.logical_and(jnp.logical_not(single), tile == (S // TILE) // 2 - 1))
    return jnp.logical_or(e == image, jnp.logical_and(mixed, e == 1))


def expert_kernel(
    w, role_ref, first_ref, res_ref, mix_ref, far_ref, wo_ref, wo_far_ref, wo_far_comp_ref, x_ref, cot_v,
    cols_ref, ob_ref, g2_ref, b2_ref, ub_ref, up_v, down_v,
    small_ref, mid_ref, n2_v, act_v, gpre_v, out_v, gn2_ref,
    mix_v, wo_v, xhat_v, gn2_v,
):
    experts = up_v.shape[0]
    width = mix_ref.shape[0] // 2
    tiles = S // TILE
    for j in range(4):
        at = pl.ds(pl.multiple_of(role_ref[3 + j] * width, width), width)
        piece = slice((j % 2) * width, (j % 2 + 1) * width)
        mix_v[at, :] = (mix_ref, far_ref)[j // 2][piece, :]
        wo_v[at, :] = wo_ref[piece, :] if j < 2 else (wo_far_ref, wo_far_comp_ref)[j - 2][...]
    expert = cols_ref[:, 0:1]
    small_ref[...] = jnp.zeros_like(small_ref)
    proj = mm(mix_v[...], wo_v[...], TN)
    middle = x_ref[...].astype(F32) + (proj + ob_ref[2:3, :])
    mid_ref[...] = middle.astype(BF16)
    xhat, _ = layer_norm(middle)
    xhat_v[...] = xhat
    n2_v[...] = (xhat * pick_rows(g2_ref, expert) + pick_rows(b2_ref, expert)).astype(BF16)

    def tile_step(tile, carry):
        at = pl.ds(pl.multiple_of(tile * TILE, TILE), TILE)
        for ref in (act_v, gpre_v, out_v, gn2_v):
            ref[at, :] = jnp.zeros((TILE, ref.shape[1]), BF16)

        def step(e, carry):
            @pl.when(present(first_ref, res_ref, w, tile, e))
            def _():
                mask = (cols_ref[at, 0:1] == e.astype(F32)).astype(F32)
                cot = cot_v[at, :]
                pre = mm(n2_v[at, :], up_v[e]) + ub_ref[pl.ds(e, 1), :]
                cdf = 0.5 + 0.5 * lax.erf(pre * (1.0 / math.sqrt(2.0)))
                act = (pre * cdf * mask).astype(BF16)
                slope = cdf + pre * (jnp.exp(-0.5 * pre * pre) * (1.0 / math.sqrt(2.0 * math.pi)))
                gpre = (mm(cot, down_v[e], NT) * slope * mask).astype(BF16)
                gn2 = mm(gpre, up_v[e], NT)
                out = mm(act, down_v[e])
                act_v[at, :] = act_v[at, :] + act
                gpre_v[at, :] = gpre_v[at, :] + gpre
                out_v[at, :] = out_v[at, :] + out.astype(BF16)
                gn2_v[at, :] = gn2_v[at, :] + gn2.astype(BF16)
                for j, values in enumerate(
                    (gn2 * xhat_v[at, :], gn2, gpre.astype(F32), cot.astype(F32) * mask)
                ):
                    row = pl.ds(j * experts + e, 1)
                    small_ref[row, :] = small_ref[row, :] + jnp.sum(values, 0, keepdims=True)

            return carry

        lax.fori_loop(0, experts, step, 0)
        return carry

    lax.fori_loop(0, tiles, tile_step, 0)
    gn2_ref[...] = gn2_v[0:BACK, :]


def expert_fwd_bwd(w, role, first, res, mix, far, wo, x, cot, cols, ob, g2, b2, ub, up, down):
    rows, model = x.shape
    experts, _, hidden = up.shape
    return pl.pallas_call(
        functools.partial(expert_kernel, w),
        out_shape=(
            jax.ShapeDtypeStruct((4 * experts, model), F32),
            jax.ShapeDtypeStruct((rows, model), BF16),
            jax.ShapeDtypeStruct((rows, model), BF16),
            jax.ShapeDtypeStruct((rows, hidden), BF16),
            jax.ShapeDtypeStruct((rows, hidden), BF16),
            jax.ShapeDtypeStruct((rows, model), BF16),
            jax.ShapeDtypeStruct((BACK, model), BF16),
        ),
        in_specs=[SMEM] * 3 + [VMEM] * 14,
        out_specs=(VMEM,) * 7,
        scratch_shapes=[
            pltpu.VMEM((rows, model), BF16),
            pltpu.VMEM((rows, model), BF16),
            pltpu.VMEM((rows, model), F32),
            pltpu.VMEM((rows, model), BF16),
        ],
        compiler_params=params(22),
        cost_estimate=cost(1e11),
        name="expert_fwd_bwd",
    )(role, first, res, mix, far, *wo, x, cot, cols, ob, g2, b2, ub, up, down)


def expert_grads_kernel(windows, first_ref, res_ref, *refs):
    groups = [refs[5 * w : 5 * w + 5] for w in range(windows)]
    out_ref, acc = refs[-2:]
    e, kind = pl.program_id(0), pl.program_id(1)
    tiles = S // TILE
    acc[...] = jnp.zeros_like(acc)

    def add(cols_ref, row, count, left, right):
        at = pl.ds(pl.multiple_of(row, TILE), count)
        mask = (cols_ref[at, 0:1] == e.astype(F32)).astype(BF16)
        acc[...] += mm(left[at, :], right[at, :] * mask, TN)

    def half_step(w, half, carry):
        n2_ref, act_ref, gpre_ref, cot_ref, cols_ref = groups[w]
        tile = 2 * half
        row = tile * TILE
        here = present(first_ref, res_ref, w, tile, e)
        next_ = present(first_ref, res_ref, w, tile + 1, e)
        for k, (left, right) in enumerate(((n2_ref, gpre_ref), (cot_ref, act_ref))):

            @pl.when(jnp.logical_and(kind == k, jnp.logical_and(here, next_)))
            def _():
                add(cols_ref, row, 2 * TILE, left, right)

            @pl.when(jnp.logical_and(kind == k, here != next_))
            def _():
                add(cols_ref, row + jnp.where(here, 0, TILE), TILE, left, right)

        return carry

    for w in range(windows):
        lax.fori_loop(0, tiles // 2, functools.partial(half_step, w), 0)
    out_ref[...] = acc[...].astype(BF16)


def expert_grads(first, res, groups, experts):
    model = groups[0][0].shape[1]
    hidden = groups[0][1].shape[1]
    flat = [a for g in groups for a in g]
    return pl.pallas_call(
        functools.partial(expert_grads_kernel, len(groups)),
        grid=(experts, 2),
        out_shape=jax.ShapeDtypeStruct((model, 2 * experts * hidden), BF16),
        in_specs=[SMEM] * 2 + [VMEM] * len(flat),
        out_specs=pl.BlockSpec((model, hidden), lambda e, k: (0, k * experts + e)),
        scratch_shapes=[pltpu.VMEM((model, hidden), F32)],
        compiler_params=params(9),
        cost_estimate=cost(1e11),
        name="expert_grads",
    )(first, res, *flat)


def mid_back_kernel(s_ref, r_ref, mid_ref, cot_ref, cols_ref, g2_ref, ga_ref):
    top = slice(0, BACK)
    total = s_ref[...].astype(F32) + r_ref[...].astype(F32)
    xhat, rstd = layer_norm(mid_ref[top, :].astype(F32))
    gain = pick_rows(g2_ref, cols_ref[top, 0:1])
    grad = cot_ref[top, :].astype(F32) + norm_back(total * gain, xhat, rstd)
    ga_ref[...] = grad.astype(BF16)


def mid_back(s, r, mid, cot, cols, g2):
    return pl.pallas_call(
        mid_back_kernel,
        out_shape=jax.ShapeDtypeStruct(s.shape, BF16),
        in_specs=[VMEM] * 6,
        out_specs=VMEM,
        compiler_params=params(10),
        cost_estimate=cost(1e11),
        name="mid_back",
    )(s, r, mid, cot, cols, g2)


def attn_bwd_kernel(
    role_ref, ga_ref, far_ref, cols_ref, wt_ref, wo_ref, mix_ref, qkv_ref, lse_ref,
    gn1_ref, dqkv_ref, gaf_ref, gmt_v,
):
    width = wo_ref.shape[0] // 2
    wide = 3 * width
    heads = width // HEAD_DIM
    take = role_ref[0] > 0
    top = pl.ds(0, BACK)

    @pl.when(take)
    def _():
        gaf_ref[top, :] = far_ref[...]

    @pl.when(jnp.logical_not(take))
    def _():
        gaf_ref[top, :] = ga_ref[...]

    gaf_ref[BACK:, :] = jnp.zeros((S - BACK, gaf_ref.shape[1]), BF16)
    gmt_v[...] = mm(wo_ref[...], gaf_ref[...], NT).astype(BF16)
    half = S // 2

    def head(i, carry):
        g, h = i // heads, lax.rem(i, heads)
        into = role_ref[1 + g] * wide
        at = lambda base: pl.ds(pl.multiple_of(base + h * HEAD_DIM, HEAD_DIM), HEAD_DIM)
        both = at(g * width)
        q_rows, k_rows, v_rows = (at(g * wide + j * width) for j in range(3))
        q_into, k_into, v_into = (at(into + j * width) for j in range(3))
        kt, vt = qkv_ref[k_rows, :], qkv_ref[v_rows, :]
        k, v = kt.T, vt.T
        row = pl.ds(i, 1)
        dk = dv = None
        for c in range(2):
            part = pl.ds(c * half, half)
            qt = qkv_ref[q_rows, part]
            dot = gmt_v[both, part]
            delta = jnp.sum(dot.astype(F32) * mix_ref[both, part].astype(F32), 0, keepdims=True)
            s = mm(k, qt) + cols_ref[:, c + 1 : c + 2]
            p = jnp.exp(s - lse_ref[row, part])
            ds = (p * (mm(v, dot) - delta)).astype(BF16)
            dv_c = mm(p.astype(BF16), dot, NT)
            dk_c = mm(ds, qt, NT)
            dv = dv_c if dv is None else dv + dv_c
            dk = dk_c if dk is None else dk + dk_c
            dqkv_ref[q_into, part] = (mm(kt, ds) * SCALE).astype(BF16)
        dqkv_ref[k_into, :] = dk.astype(BF16).T
        dqkv_ref[v_into, :] = dv.astype(BF16).T
        return carry

    lax.fori_loop(0, 2 * heads, head, 0)
    gn1_ref[...] = mm(dqkv_ref[:, 0:BACK], wt_ref[...], TN).astype(BF16)


def attn_bwd(role, ga, far, cols, wt, wo, mix, qkv, lse):
    model = wo.shape[1]
    return pl.pallas_call(
        attn_bwd_kernel,
        out_shape=(
            jax.ShapeDtypeStruct((BACK, model), BF16),
            jax.ShapeDtypeStruct(qkv.shape, BF16),
            jax.ShapeDtypeStruct((S, model), BF16),
        ),
        in_specs=[SMEM] + [VMEM] * 8,
        out_specs=(VMEM,) * 3,
        scratch_shapes=[pltpu.VMEM(mix.shape, BF16)],
        compiler_params=params(11),
        cost_estimate=cost(1e11),
        name="attn_bwd",
    )(role, ga, far, cols, wt, wo, mix, qkv, lse)


def attn_grads_kernel(role_ref, *refs):
    windows = (len(refs) - 8) // 4
    groups = [refs[4 * w : 4 * w + 4] for w in range(windows)]
    out_ref, sum_ref, n1_v, gaf_v, dqkv_v, mix_v, acc, sems = refs[-8:]
    wide = dqkv_v.shape[0]
    own = pl.ds(pl.multiple_of(role_ref[1] * wide, wide), wide)
    loads = []
    for w, (n1_ref, dqkv_ref, mix_ref, gaf_ref) in enumerate(groups):
        at = pl.ds(w * S, S)
        pairs = (
            (dqkv_ref.at[own, :], dqkv_v.at[:, at]),
            (n1_ref, n1_v.at[at, :]),
            (mix_ref.at[pl.ds(0, mix_v.shape[0]), :], mix_v.at[:, at]),
            (gaf_ref, gaf_v.at[at, :]),
        )
        loads += [start(a, b, sems.at[4 * w + j]) for j, (a, b) in enumerate(pairs)]
    for load in loads:
        load.wait()
    acc[0:wide, :] = mm(dqkv_v[...], n1_v[...])
    acc[wide:, :] = mm(mix_v[...], gaf_v[...])
    sum_ref[...] = mm(jnp.ones((8, dqkv_v.shape[1]), BF16), dqkv_v[...], NT)
    out_ref[...] = acc[...].astype(BF16).T


def attn_grads(role, groups):
    n1, dqkv = groups[0][:2]
    model = n1.shape[1]
    wide = dqkv.shape[0] // 2
    rows = len(groups) * S
    flat = [a for g in groups for a in g]
    outs = (
        jax.ShapeDtypeStruct((model, wide + wide // 3), BF16),
        jax.ShapeDtypeStruct((8, wide), F32),
    )
    return pl.pallas_call(
        attn_grads_kernel,
        grid=(1,),
        out_shape=outs,
        in_specs=[SMEM] + [HBM] * len(flat),
        out_specs=tuple(full(o) for o in outs),
        scratch_shapes=[
            pltpu.VMEM((rows, model), BF16),
            pltpu.VMEM((rows, model), BF16),
            pltpu.VMEM((wide, rows), BF16),
            pltpu.VMEM((wide // 3, rows), BF16),
            pltpu.VMEM((wide + wide // 3, model), F32),
            pltpu.SemaphoreType.DMA((4 * len(groups),)),
        ],
        compiler_params=params(50),
        cost_estimate=cost(1e11),
        name="attn_grads",
    )(role, *flat)


def first_back_kernel(w, s_ref, r_ref, ga_ref, x_ref, g_ref, *refs):
    out_ref, sum_ref, out_v, sem = refs[-4:]
    top = slice(0, BACK)
    total = s_ref[...].astype(F32) + r_ref[...].astype(F32)
    xhat, rstd = layer_norm(x_ref[top, :].astype(F32))
    ga = ga_ref[top, :].astype(F32)
    back = norm_back(total * g_ref[0:1, :], xhat, rstd)
    out_v[top, :] = (ga + back).astype(BF16)
    out_v[BACK:, :] = jnp.zeros((S - BACK, out_v.shape[1]), BF16)
    copy = start(out_v, out_ref.at[pl.ds(w * S, S), :], sem)
    sum_ref[...] = jnp.zeros_like(sum_ref)
    for j, values in enumerate((total * xhat, total, ga)):
        sum_ref[j : j + 1, :] = jnp.sum(values, 0, keepdims=True)
    copy.wait()


def first_back(w, s, r, ga, x, g, rows, into):
    model = s.shape[1]
    more = () if into is None else (into,)
    return pl.pallas_call(
        functools.partial(first_back_kernel, w),
        out_shape=(
            jax.ShapeDtypeStruct((rows, model), BF16),
            jax.ShapeDtypeStruct((8, model), F32),
        ),
        in_specs=[VMEM] * 5 + [HBM] * len(more),
        out_specs=(HBM, VMEM),
        scratch_shapes=[pltpu.VMEM((S, model), BF16), pltpu.SemaphoreType.DMA],
        input_output_aliases={5: 0} if more else {},
        compiler_params=params(12),
        cost_estimate=cost(1e11),
        name="first_back",
    )(s, r, ga, x, g, *more)


def layer_out_kernel(s_ref, r_ref, mid_ref, cols_ref, db_ref, out_ref):
    total = s_ref[...].astype(F32) + r_ref[...].astype(F32)
    shift = pick_rows(db_ref, cols_ref[:, 0:1])
    out_ref[...] = (mid_ref[...].astype(F32) + (total + shift)).astype(BF16)


def layer_out_rows(s, r, mid, cols, db):
    return pl.pallas_call(
        layer_out_kernel,
        out_shape=jax.ShapeDtypeStruct(mid.shape, BF16),
        in_specs=[VMEM] * 5,
        out_specs=VMEM,
        compiler_params=params(10),
        cost_estimate=cost(1e11),
        name="layer_out_rows",
    )(s, r, mid, cols, db)


def place_kernel(w, role_ref, own_ref, far_ref, *refs):
    out_ref, out_v, sem = refs[-3:]

    @pl.when(role_ref[0] > 0)
    def _():
        out_v[...] = far_ref[...]

    @pl.when(role_ref[0] == 0)
    def _():
        out_v[...] = own_ref[...]

    start(out_v, out_ref.at[pl.ds(w * S, S), :], sem).wait()


def place_rows(w, role, own, far, rows, into):
    model = own.shape[1]
    more = () if into is None else (into,)
    return pl.pallas_call(
        functools.partial(place_kernel, w),
        out_shape=jax.ShapeDtypeStruct((rows, model), BF16),
        in_specs=[SMEM] + [VMEM] * 2 + [HBM] * len(more),
        out_specs=HBM,
        scratch_shapes=[pltpu.VMEM((S, model), BF16), pltpu.SemaphoreType.DMA],
        input_output_aliases={3: 0} if more else {},
        compiler_params=params(5),
        cost_estimate=cost(1e11),
        name="place_rows",
    )(role, own, far, *more)


def inward(v):
    return lax.ppermute(v, "tensor", [(0, 1), (3, 2)])


def across(v):
    return lax.ppermute(v, "tensor", [(1, 2), (2, 1)])


def outward(v):
    return lax.ppermute(v, "tensor", [(1, 0), (2, 3)])


def swap(v, axis, bit):
    return lax.ppermute(v, axis, [(i, i ^ bit) for i in range(lax.axis_size(axis))])


def add_rounded(a, b):
    return (a.astype(F32) + b.astype(F32)).astype(BF16)


def after(first, value):
    return lax.optimization_barrier((first, value))[1]


class Order:
    def __init__(self):
        self.last = None

    def __call__(self, step, value, *rest):
        if self.last is not None:
            value = after(self.last, value)
        out = step(value, *rest)
        leaves = jax.tree.leaves(out)
        self.last = min(leaves, key=lambda a: a.size)
        return out


def halve(value, left, bit, run):
    axis, mine = left.index(bit), (lax.axis_index("dp") >> bit) & 1
    sent = run(lambda v: lax.dynamic_index_in_dim(v, 1 - mine, axis, keepdims=False), value)
    got = swap(sent, "dp", 1 << bit)

    def add(got, value):
        return add_rounded(lax.dynamic_index_in_dim(value, mine, axis, keepdims=False), got)

    return value, got, add, [b for b in left if b != bit]


class ScatterSum:
    def __init__(self, value, widths, run):
        self.run, self.widths = run, widths
        count = lax.axis_size("dp")
        bits = count.bit_length() - 1
        rows, columns = value.shape
        value = value.reshape((2,) * bits + (rows // count, columns))
        self.parts = [(halve(value, list(range(bits - 1, -1, -1)), 0, run), 1)]

    def add(self):
        values = [(self.run(h[2], h[1], h[0]), h[3], way) for h, way in self.parts]
        if self.widths:
            value, left, _ = values[0]
            ends = [sum(self.widths[: k + 1]) for k in range(len(self.widths))]
            values = [
                (value[..., e - n : e], left, (-1) ** k)
                for k, (e, n) in enumerate(zip(ends, self.widths))
            ]
            self.widths = None
        if not values[0][1]:
            return [v.astype(F32) for v, _, _ in values]
        self.parts = [
            (halve(v, left, left[::-way][0], self.run), way) for v, left, way in values
        ]
        return None

    def finish(self):
        done = None
        while done is None:
            done = self.add()
        return done


def body(
    inputs, cotangent, row_expert, row_keep, window_resolution, attention_norm_gain,
    attention_norm_bias, qkv_weight, qv_bias, out_weight, out_bias, second_gain,
    expert_norm_bias, up_weight, up_bias, down_weight, down_bias,
):
    row_count, model = inputs.shape
    experts = up_weight.shape[0]
    width = qkv_weight.shape[2]
    windows = row_count // S
    tiles = S // TILE
    me = lax.axis_index("tensor")
    low = me < 2
    at_end = (me == 0) | (me == 3)
    place = lax.axis_index("dp")
    turn = ((place >> 1) & 1) + 2 * (place & 1)
    role = jnp.concatenate(
        [
            jnp.asarray(ROLES, jnp.int32)[me],
            turn ^ jnp.arange(4, dtype=jnp.int32),
        ]
    )
    run = Order()

    wt = jnp.transpose(qkv_weight, (0, 2, 1)).reshape(3 * width, model)
    pack = jnp.concatenate([wt, out_weight], 0)
    part = lax.dynamic_slice_in_dim(pack, turn * width, width, 0)
    part = swap(part, "tensor", 2)
    wo_far = swap(out_weight, "tensor", 1)
    wb = qv_bias.reshape(2, width)
    wb_c = swap(wb, "tensor", 2)
    every = range(windows)
    expert_rows, keep_rows = row_expert.reshape(windows, S), row_keep.reshape(windows, S)
    consts = jnp.stack([attention_norm_gain, attention_norm_bias, out_bias])
    at = [slice(w * S, (w + 1) * S) for w in every]
    xs, cots = [inputs[at[0]], None, None], [None] * windows

    given = (expert_rows, keep_rows, consts, wt, wb)
    own_lse, n1, own_qkv, own_mix, facts = run(
        lambda x: attn_own(0, window_resolution, x, *given), xs[0]
    )
    part = after(wo_far, after(wb_c, after(run.last, part)))
    beside = swap(part, "dp", 2)
    across_core = swap(part, "dp", 1)
    for w in every:
        cots[w] = run(lambda c: c[at[w]], cotangent)
    first = run(lambda e: e[:: S // 2], row_expert)
    beside = after(run.last, beside)
    last = swap(beside, "dp", 1)
    for w in (1, 2):
        xs[w] = run(lambda c: c[at[w]], inputs)
    lse, qkv, mix, wt_c, wt_both, wo_both, wo_c = run(
        lambda f: attn_comp(
            role, (part, beside, across_core, f), wt, out_weight, (own_lse, n1, own_qkv, own_mix), facts, wb_c
        ),
        last,
    )
    wo = (wo_both, wo_far, swap(wo_c, "tensor", 1))
    fwd = [(lse, n1, qkv, mix, facts)]
    mix_far = [swap(mix, "tensor", 1)]
    for w in (1, 2):
        fwd.append(run(lambda x: attn_both(w, window_resolution, x, *given, wt_c, wb_c), xs[w]))
        mix_far.append(swap(fwd[w][3], "tensor", 1))
    cols = [fwd[w][4] for w in every]

    ex, gn2_in, s2, ga, bwd = ([None] * windows for _ in range(5))
    part_in, s_out, lo, sums = ([None] * windows for _ in range(4))

    def do_experts(w):
        def step(far_mix):
            return expert_fwd_bwd(
                w, role, first, window_resolution, fwd[w][3], far_mix, wo, xs[w],
                cots[w], cols[w], consts, second_gain, expert_norm_bias, up_bias, up_weight, down_weight,
            )

        ex[w] = run(step, mix_far[w])
        gn2_in[w] = inward(ex[w][6])

    def do_sum2(w):
        s2[w] = run(add_rounded, gn2_in[w], ex[w][6])

    def do_mid(w):
        ga[w] = run(
            lambda r: mid_back(s2[w], r, ex[w][1], cots[w], cols[w], second_gain), across(s2[w])
        )

    def do_bwd(w):
        lse, _, qkv, mix, _ = fwd[w]
        bwd[w] = run(
            lambda far: attn_bwd(role, ga[w], far, cols[w], wt_both, wo_both, mix, qkv, lse),
            outward(ga[w]),
        )

    def do_first(w, into):
        gn1, _, gaf = bwd[w]
        into, sums[w] = run(
            lambda r: first_back(w, gn1, r, gaf, xs[w], consts, row_count, into),
            swap(gn1, "tensor", 1),
        )
        return into

    def do_place(w, into):
        return run(lambda f: place_rows(w, role, lo[w], f, row_count, into), outward(lo[w]))

    def start_out(w):
        part_in[w] = inward(after(run.last, ex[w][5]))

    def do_out_sum(w):
        s_out[w] = run(add_rounded, part_in[w], ex[w][5])

    def do_out(w):
        lo[w] = run(
            lambda r: layer_out_rows(s_out[w], r, ex[w][1], cols[w], down_bias), across(s_out[w])
        )

    do_experts(0)
    do_experts(1)
    do_sum2(0)
    do_experts(2)
    start_out(0)
    small = run(lambda a, b, c: a + b + c, ex[2][0], ex[0][0], ex[1][0])
    shared = small[: 2 * experts]
    other = swap(shared, "tensor", 1)
    do_sum2(1)
    do_mid(0)
    do_sum2(2)
    do_mid(1)
    do_bwd(0)
    shared = run(lambda o: shared + o, other)
    other = swap(shared, "tensor", 2)
    start_out(1)
    do_out_sum(0)
    do_mid(2)
    do_bwd(1)
    shared = run(lambda o: shared + o, other)
    do_out(0)
    grad_rows = do_first(0, None)
    do_out_sum(1)
    start_out(2)
    do_bwd(2)
    grad_rows = do_first(1, grad_rows)
    do_out(1)
    groups = [(*ex[w][2:5], cots[w], cols[w]) for w in every]
    expert_g = run(lambda f: expert_grads(f, window_resolution, groups, experts), first)
    hidden = up_weight.shape[2]
    eg = ScatterSum(expert_g, (experts * hidden, experts * hidden), run)
    do_out_sum(2)
    out_rows = do_place(0, None)
    eg.add()
    grad_rows = do_first(2, grad_rows)
    groups = [(fwd[w][1], bwd[w][1], fwd[w][3], bwd[w][2]) for w in every]
    attn_g, col_sums = run(lambda r: attn_grads(r, groups), role)
    do_out(2)
    eg.add()
    ag = ScatterSum(attn_g, (4 * width,), run)
    out_rows = do_place(1, out_rows)
    ag.add()
    up_g, down_g = eg.finish()
    ag.add()
    totals = jnp.concatenate(
        [
            shared,
            small[2 * experts :],
            (sums[0] + sums[1] + sums[2])[:3],
            jnp.pad(col_sums[:1], ((0, 0), (0, model - 3 * width))),
        ],
        0,
    )
    totals = after(run.last, totals)
    for b in range(lax.axis_size("dp").bit_length() - 1):
        totals = totals + swap(totals, "dp", 1 << b)
    (attn_g,) = ag.finish()
    block = up_g.shape[0]
    grad_up = jnp.transpose(up_g.reshape(block, experts, hidden), (1, 0, 2))
    grad_down = jnp.transpose(down_g.reshape(block, experts, hidden), (1, 2, 0))
    grad_qkv = jnp.transpose(attn_g[:, : 3 * width].reshape(block, 3, width), (1, 0, 2))
    grad_out = attn_g[:, 3 * width :].T
    col = totals[4 * experts + 3]
    qv_grad = jnp.stack([col[:width], col[2 * width : 3 * width]]).reshape(qv_bias.shape)
    return (
        do_place(2, out_rows),
        grad_rows,
        totals[4 * experts],
        totals[4 * experts + 1],
        grad_qkv,
        qv_grad,
        grad_out,
        totals[4 * experts + 2],
        totals[:experts],
        totals[experts : 2 * experts],
        grad_up,
        totals[2 * experts : 3 * experts],
        grad_down,
        totals[3 * experts : 4 * experts],
    )


def solution(mesh):
    in_specs = (
        P("dp", None), P("dp", None), P("dp"), P("dp"), P("dp"), P(), P(),
        P(None, None, "tensor"), P(None, "tensor", None), P("tensor", None), P(), P(), P(),
        P(None, None, "tensor"), P(None, "tensor"), P(None, "tensor", None), P(),
    )
    out_specs = (
        P("dp", None), P("dp", None), P(), P(), P(None, "dp", "tensor"), P(None, "tensor", None),
        P("tensor", "dp"), P(), P(), P(), P(None, "dp", "tensor"), P(None, "tensor"),
        P(None, "tensor", "dp"), P(),
    )
    return jax.shard_map(body, mesh=mesh, in_specs=in_specs, out_specs=out_specs, check_vma=False)
```
